768 devices in a mesh: mode: 16 (over x_hi, y), tile: 48 (over z, x_lo, core).
Axes of the slice: x: 4 (x_hi: 2, x_lo: 2; x = x_hi * 2 + x_lo), y: 8, z: 12, core: 2. Of those that a mesh axis runs over, the one named last changes fastest.
Arguments:
- velocity: float32 [128, 3, 196608], P('mode', None, 'tile'), may hold values from -6 to 6
- vorticity: float32 [128, 3, 196608], P('mode', None, 'tile'), may hold values from -6 to 6
- viscosity: float32 [2], replicated, may hold values from 0.1 to 0.4
Outputs:
- rate: float32 [128, 3, 196608], P('mode', None, 'tile')
The draws below stay inside these ranges and needn't reach their ends.
All inputs are finite; a program needn't handle non-finite values.
Results may differ from the reference program's by a relative error of at most 0.0001.
Values sent between devices are 32-bit elements; how exact they have to be, the bound alone decides.
A program may use at most 32 MiB of HBM per device.

```python
import math
import jax
import jax.numpy as jnp
import numpy as np
from jax import lax

MODES = 8
NY = 1024
NZ = 16
NX = 192


def block_scale(stream_key, shape, pieces, low, largest):
    gain = 1.0
    for position, shards_of in pieces:
        steps = jax.random.uniform(jax.random.fold_in(jax.random.fold_in(stream_key, 6), position), (shards_of,), jnp.float32, low / len(pieces), largest / len(pieces))
        gain = gain * jnp.repeat(jnp.exp(steps), shape[position] // shards_of).reshape((-1,) + (1,) * (len(shape) - 1 - position))
    return gain


def noise(key, extent, spread, reach, split=(), held_as=jnp.bfloat16):
    drawn = spread * jax.random.normal(key, extent, jnp.float32)
    if split:
        drawn = drawn * block_scale(key, extent, split, -0.22, 0.18)
    return jnp.clip(drawn, -reach, reach).astype(held_as)


def setup_inputs(seed: int = 0) -> dict:
    key_of = jax.random.split(jax.random.key(seed), 4)
    velocity = noise(key_of[0], (MODES * NZ, 3, NX * NY), 1.0, 6.0, ((0, 16), (2, 48)), jnp.float32)
    vorticity = noise(key_of[1], (MODES * NZ, 3, NX * NY), 1.0, 6.0, ((0, 16), (2, 48)), jnp.float32)
    viscosity = jnp.clip(jax.random.uniform(key_of[2], (2,), jnp.float32, 0.1, 0.4), 0.1, 0.4)
    return dict(velocity=velocity, vorticity=vorticity, viscosity=viscosity)


def legendre_list(count, where):
    values_list = [1.0, where]
    for degree in range(1, count):
        values_list.append(((2 * degree + 1) * where * values_list[degree] - degree * values_list[degree - 1]) / (degree + 1))
    return values_list

def gauss_nodes(order):
    nodes_list = []
    weights_list = []
    for number in range(order):
        guess = math.cos(math.pi * (number + 0.75) / (order + 0.5))
        for sweep in range(60):
            values_list = legendre_list(order, guess)
            slope = order * (guess * values_list[order] - values_list[order - 1]) / (guess * guess - 1.0)
            guess = guess - values_list[order] / slope
        values_list = legendre_list(order, guess)
        slope = order * (guess * values_list[order] - values_list[order - 1]) / (guess * guess - 1.0)
        nodes_list.append(guess)
        weights_list.append(2.0 / ((1.0 - guess * guess) * slope * slope))
    return (nodes_list, weights_list)

def triple_table(mode_count):
    nodes_list, weights_list = gauss_nodes(2 * mode_count)
    scaled = [[math.sqrt(2.0 * degree + 1.0) * legendre_list(mode_count, node_value)[degree] for degree in range(mode_count)] for node_value in nodes_list]
    table = [[[0.5 * sum((weights_list[number] * scaled[number][first] * scaled[number][second] * scaled[number][third] for number in range(len(nodes_list)))) for third in range(mode_count)] for second in range(mode_count)] for first in range(mode_count)]
    return np.array(table)

def cross_along(left_vec, right_vec, direction):

    def component(vector, number):
        return lax.index_in_dim(vector, number, direction, keepdims=False)
    components = [component(left_vec, 1) * component(right_vec, 2) - component(left_vec, 2) * component(right_vec, 1), component(left_vec, 2) * component(right_vec, 0) - component(left_vec, 0) * component(right_vec, 2), component(left_vec, 0) * component(right_vec, 1) - component(left_vec, 1) * component(right_vec, 0)]
    return jnp.stack(components, axis=direction)

def centred(source_field, direction):
    return 0.5 * (jnp.roll(source_field, -1, direction) - jnp.roll(source_field, 1, direction))

def second_diff(source_field, direction):
    return jnp.roll(source_field, -1, direction) + jnp.roll(source_field, 1, direction) - 2.0 * source_field

def reference(velocity, vorticity, viscosity):
    coupling = jnp.asarray(triple_table(MODES), dtype=jnp.float32)
    mixing = viscosity[0] * coupling[0] + viscosity[1] * coupling[1]
    speed_modes = velocity.reshape(MODES, NZ, 3, NX, NY)
    spin_modes = vorticity.reshape(MODES, NZ, 3, NX, NY)

    def one_mode(target):
        pairs = lax.dynamic_index_in_dim(coupling, target, 2, keepdims=False)
        flux_terms = jnp.zeros((NZ, 3, NX, NY), jnp.float32)
        for source in range(MODES):
            mixed_spin = jnp.tensordot(pairs[source], spin_modes, axes=1, precision=lax.Precision.HIGHEST)
            flux_terms = flux_terms + cross_along(speed_modes[source], mixed_spin, 1)
        column = lax.dynamic_index_in_dim(mixing, target, 1, keepdims=False)
        damped = jnp.tensordot(column, spin_modes, axes=1, precision=lax.Precision.HIGHEST)
        flux_x = flux_terms[:, 0]
        flux_y = flux_terms[:, 1]
        flux_z = flux_terms[:, 2]
        curl_x = centred(flux_z, 2) - centred(flux_y, 0)
        curl_y = centred(flux_x, 0) - centred(flux_z, 1)
        curl_z = centred(flux_y, 1) - centred(flux_x, 2)
        laplace = second_diff(damped, 0) + second_diff(damped, 2) + second_diff(damped, 3)
        return jnp.stack([curl_x, curl_y, curl_z], axis=1) + laplace
    rates = lax.map(one_mode, jnp.arange(MODES, dtype=jnp.int32))
    return rates.reshape(MODES * NZ, 3, NX * NY)
```

```python
import math

import jax
import jax.numpy as jnp
import numpy as np
from jax import lax
from jax.sharding import PartitionSpec as P

MODES = 8
NY = 1024


def padded(block, sides, width):
    for axis, dim in sides:
        count = lax.axis_size(axis)
        forward = [(i, i + 1) for i in range(count - 1)]
        forward.append((count - 1, 0))
        backward = [(target, source) for source, target in forward]
        low = lax.ppermute(
            lax.slice_in_dim(block, block.shape[dim] - width, None, axis=dim), axis, forward
        )
        high = lax.ppermute(lax.slice_in_dim(block, 0, width, axis=dim), axis, backward)
        block = jnp.concatenate([low, block, high], axis=dim)
    return block


def legendre_list(count, where):
    values_list = [1.0, where]
    for degree in range(1, count):
        values_list.append(
            ((2 * degree + 1) * where * values_list[degree] - degree * values_list[degree - 1])
            / (degree + 1)
        )
    return values_list


def gauss_nodes(order):
    nodes_list = []
    weights_list = []
    for number in range(order):
        guess = math.cos(math.pi * (number + 0.75) / (order + 0.5))
        for sweep in range(60):
            values_list = legendre_list(order, guess)
            slope = (
                order
                * (guess * values_list[order] - values_list[order - 1])
                / (guess * guess - 1.0)
            )
            guess = guess - values_list[order] / slope
        values_list = legendre_list(order, guess)
        slope = (
            order * (guess * values_list[order] - values_list[order - 1]) / (guess * guess - 1.0)
        )
        nodes_list.append(guess)
        weights_list.append(2.0 / ((1.0 - guess * guess) * slope * slope))
    return (nodes_list, weights_list)


def triple_table(mode_count):
    nodes_list, weights_list = gauss_nodes(2 * mode_count)
    scaled = [
        [
            math.sqrt(2.0 * degree + 1.0) * legendre_list(mode_count, node_value)[degree]
            for degree in range(mode_count)
        ]
        for node_value in nodes_list
    ]
    table = [
        [
            [
                0.5
                * sum(
                    (
                        weights_list[number]
                        * scaled[number][first]
                        * scaled[number][second]
                        * scaled[number][third]
                        for number in range(len(nodes_list))
                    )
                )
                for third in range(mode_count)
            ]
            for second in range(mode_count)
        ]
        for first in range(mode_count)
    ]
    return np.array(table)


def cross_along(left_vec, right_vec, direction):

    def component(vector, number):
        return lax.index_in_dim(vector, number, direction, keepdims=False)

    components = [
        component(left_vec, 1) * component(right_vec, 2)
        - component(left_vec, 2) * component(right_vec, 1),
        component(left_vec, 2) * component(right_vec, 0)
        - component(left_vec, 0) * component(right_vec, 2),
        component(left_vec, 0) * component(right_vec, 1)
        - component(left_vec, 1) * component(right_vec, 0),
    ]
    return jnp.stack(components, axis=direction)


def centred(source_field, direction):
    return 0.5 * (jnp.roll(source_field, -1, direction) - jnp.roll(source_field, 1, direction))


def second_diff(source_field, direction):
    return (
        jnp.roll(source_field, -1, direction)
        + jnp.roll(source_field, 1, direction)
        - 2.0 * source_field
    )


def pack_rows(block):
    lead = block.shape[0]
    return block.reshape(lead, -1, 128)


def shards(velocity, vorticity, viscosity):
    row_count = velocity.shape[0]
    cell_count = velocity.shape[2]
    slab_rows = cell_count // NY
    group_count = lax.axis_size("mode")
    chunk = NY // group_count
    planes = row_count * group_count // MODES
    coupling = jnp.asarray(triple_table(MODES), dtype=jnp.float32)
    mixing = viscosity[0] * coupling[0] + viscosity[1] * coupling[1]
    flat_coupling = jnp.transpose(coupling, (0, 2, 1)).reshape(MODES * MODES, MODES)
    mixing_rows = jnp.transpose(mixing)

    def windows(source_field):
        main = source_field.reshape(row_count, 3, slab_rows, group_count, chunk)
        left = jnp.roll(main[..., chunk - 1], 1, axis=3)[..., None]
        right = jnp.roll(main[..., 0], -1, axis=3)[..., None]
        return jnp.concatenate([left, main, right], axis=4)

    both = jnp.stack([windows(velocity), windows(vorticity)], axis=0)
    both = jnp.transpose(both, (4, 0, 1, 2, 3, 5))
    wide = chunk + 2
    arrived = lax.all_to_all(pack_rows(both), "mode", split_axis=0, concat_axis=0, tiled=True)
    arrived = arrived.reshape(MODES, group_count // MODES, 2, row_count, 3, slab_rows, wide)
    arrived = jnp.transpose(arrived, (2, 0, 1, 3, 4, 5, 6)).reshape(
        2, MODES, planes, 3, slab_rows, wide
    )
    speed = arrived[0]
    spin_flat = arrived[1].reshape(MODES, -1)
    mixed_spin = jnp.dot(flat_coupling, spin_flat, precision=lax.Precision.HIGHEST).reshape(
        MODES, MODES, planes, 3, slab_rows, wide
    )
    flux = jnp.sum(cross_along(speed[:, None], mixed_spin, 3), axis=0)
    damped = jnp.dot(mixing_rows, spin_flat, precision=lax.Precision.HIGHEST).reshape(
        MODES, planes, 3, slab_rows, wide
    )
    fields = jnp.concatenate([flux, damped], axis=2)
    count = lax.axis_size("tile")
    forward = [(i, (i + 1) % count) for i in range(count)]
    backward = [((i + 1) % count, i) for i in range(count)]
    edge_shape = fields[:, :, :, 0].shape
    low = lax.ppermute(fields[:, :, :, slab_rows - 1].reshape(-1, 128), "tile", forward)
    high = lax.ppermute(fields[:, :, :, 0].reshape(-1, 128), "tile", backward)
    rim = jnp.concatenate(
        [low.reshape(edge_shape)[:, :, :, None], fields, high.reshape(edge_shape)[:, :, :, None]],
        axis=3,
    )

    def core(f):
        return f[:, :, 1:-1, 1:-1]

    def d_y(f):
        return 0.5 * (f[:, :, 1:-1, 2:] - f[:, :, 1:-1, :-2])

    def d_x(f):
        return 0.5 * (f[:, :, 2:, 1:-1] - f[:, :, :-2, 1:-1])

    def d_z(f):
        return centred(core(f), 1)

    def laplace(f):
        inner = core(f)
        return (
            second_diff(inner, 1)
            + (f[:, :, 2:, 1:-1] + f[:, :, :-2, 1:-1] - 2.0 * inner)
            + (f[:, :, 1:-1, 2:] + f[:, :, 1:-1, :-2] - 2.0 * inner)
        )

    flux_x = rim[:, :, 0]
    flux_y = rim[:, :, 1]
    flux_z = rim[:, :, 2]
    rate_x = d_y(flux_z) - d_z(flux_y) + laplace(rim[:, :, 3])
    rate_y = d_z(flux_x) - d_x(flux_z) + laplace(rim[:, :, 4])
    rate_z = d_x(flux_y) - d_y(flux_x) + laplace(rim[:, :, 5])
    rate = jnp.stack([rate_x, rate_y, rate_z], axis=2)
    rate = rate.reshape(group_count, -1)
    returned = lax.all_to_all(pack_rows(rate), "mode", split_axis=0, concat_axis=0, tiled=True)
    returned = returned.reshape(group_count, row_count, 3, slab_rows, chunk)
    returned = jnp.transpose(returned, (1, 2, 3, 0, 4))
    return returned.reshape(row_count, 3, cell_count)


def solution(mesh):
    in_specs = (P("mode", None, "tile"), P("mode", None, "tile"), P())
    out_specs = P("mode", None, "tile")
    return jax.shard_map(shards, mesh=mesh, in_specs=in_specs, out_specs=out_specs, check_vma=False)
```

```python
import functools
import math

import jax
import jax.numpy as jnp
import numpy as np
from jax import lax
from jax.experimental import pallas as pl
from jax.experimental.pallas import tpu as pltpu
from jax.sharding import PartitionSpec as P

MODES = 8
NY = 1024


def padded(block, sides, width):
    for axis, dim in sides:
        count = lax.axis_size(axis)
        forward = [(i, i + 1) for i in range(count - 1)]
        forward.append((count - 1, 0))
        backward = [(target, source) for source, target in forward]
        low = lax.ppermute(
            lax.slice_in_dim(block, block.shape[dim] - width, None, axis=dim), axis, forward
        )
        high = lax.ppermute(lax.slice_in_dim(block, 0, width, axis=dim), axis, backward)
        block = jnp.concatenate([low, block, high], axis=dim)
    return block


def legendre_list(count, where):
    values_list = [1.0, where]
    for degree in range(1, count):
        values_list.append(
            ((2 * degree + 1) * where * values_list[degree] - degree * values_list[degree - 1])
            / (degree + 1)
        )
    return values_list


def gauss_nodes(order):
    nodes_list = []
    weights_list = []
    for number in range(order):
        guess = math.cos(math.pi * (number + 0.75) / (order + 0.5))
        for sweep in range(60):
            values_list = legendre_list(order, guess)
            slope = (
                order
                * (guess * values_list[order] - values_list[order - 1])
                / (guess * guess - 1.0)
            )
            guess = guess - values_list[order] / slope
        values_list = legendre_list(order, guess)
        slope = (
            order * (guess * values_list[order] - values_list[order - 1]) / (guess * guess - 1.0)
        )
        nodes_list.append(guess)
        weights_list.append(2.0 / ((1.0 - guess * guess) * slope * slope))
    return (nodes_list, weights_list)


def triple_table(mode_count):
    nodes_list, weights_list = gauss_nodes(2 * mode_count)
    scaled = [
        [
            math.sqrt(2.0 * degree + 1.0) * legendre_list(mode_count, node_value)[degree]
            for degree in range(mode_count)
        ]
        for node_value in nodes_list
    ]
    table = [
        [
            [
                0.5
                * sum(
                    (
                        weights_list[number]
                        * scaled[number][first]
                        * scaled[number][second]
                        * scaled[number][third]
                        for number in range(len(nodes_list))
                    )
                )
                for third in range(mode_count)
            ]
            for second in range(mode_count)
        ]
        for first in range(mode_count)
    ]
    return np.array(table)


def cross_along(left_vec, right_vec, direction):

    def component(vector, number):
        return lax.index_in_dim(vector, number, direction, keepdims=False)

    components = [
        component(left_vec, 1) * component(right_vec, 2)
        - component(left_vec, 2) * component(right_vec, 1),
        component(left_vec, 2) * component(right_vec, 0)
        - component(left_vec, 0) * component(right_vec, 2),
        component(left_vec, 0) * component(right_vec, 1)
        - component(left_vec, 1) * component(right_vec, 0),
    ]
    return jnp.stack(components, axis=direction)


def centred(source_field, direction):
    return 0.5 * (jnp.roll(source_field, -1, direction) - jnp.roll(source_field, 1, direction))


def second_diff(source_field, direction):
    return (
        jnp.roll(source_field, -1, direction)
        + jnp.roll(source_field, 1, direction)
        - 2.0 * source_field
    )


def stencil_kernel(chunk, slab_rows, f_ref, r_ref, lo_ref, hi_ref, o_ref):
    planes, piece = f_ref.shape[2], f_ref.shape[3]
    lane = lax.broadcasted_iota(jnp.int32, (planes, piece), 1)
    y_of = lane % chunk
    x_of = lane // chunk
    first_y = y_of == 0
    last_y = y_of == chunk - 1
    first_x = x_of == 0
    last_x = x_of == slab_rows - 1

    for k in range(f_ref.shape[1]):

        def rim(c, side):
            out = jnp.zeros((planes, piece), jnp.float32)
            for row in range(slab_rows):
                out = jnp.where(x_of == row, r_ref[c, k, side, row], out)
            return out

        def moved(c, halo):
            f = f_ref[c, k]
            y_up = jnp.where(last_y, rim(c, 1), pltpu.roll(f, piece - 1, 1))
            y_down = jnp.where(first_y, rim(c, 0), pltpu.roll(f, 1, 1))
            z_up = pltpu.roll(f, planes - 1, 0)
            z_down = pltpu.roll(f, 1, 0)
            if halo is None:
                return f, y_up, y_down, z_up, z_down, None, None
            x_up = jnp.where(last_x, hi_ref[halo, k], pltpu.roll(f, piece - chunk, 1))
            x_down = jnp.where(first_x, lo_ref[halo, k], pltpu.roll(f, chunk, 1))
            return f, y_up, y_down, z_up, z_down, x_up, x_down

        def laplace(c):
            f, y_up, y_down, z_up, z_down, x_up, x_down = moved(3 + c, 2 + c)
            return (z_up + z_down - 2.0 * f) + (x_up + x_down - 2.0 * f) + (y_up + y_down - 2.0 * f)

        _, fx_yu, fx_yd, fx_zu, fx_zd, _, _ = moved(0, None)
        _, fy_yu, fy_yd, fy_zu, fy_zd, fy_xu, fy_xd = moved(1, 0)
        _, fz_yu, fz_yd, fz_zu, fz_zd, fz_xu, fz_xd = moved(2, 1)
        o_ref[k, 0] = 0.5 * (fz_yu - fz_yd) - 0.5 * (fy_zu - fy_zd) + laplace(0)
        o_ref[k, 1] = 0.5 * (fx_zu - fx_zd) - 0.5 * (fz_xu - fz_xd) + laplace(1)
        o_ref[k, 2] = 0.5 * (fy_xu - fy_xd) - 0.5 * (fx_yu - fx_yd) + laplace(2)


def shards(velocity, vorticity, viscosity):
    row_count = velocity.shape[0]
    cell_count = velocity.shape[2]
    slab_rows = cell_count // NY
    group_count = lax.axis_size("mode")
    chunk = NY // group_count
    piece = slab_rows * chunk
    halves = group_count // MODES
    planes = row_count * halves
    coupling = jnp.asarray(triple_table(MODES), dtype=jnp.float32)
    mixing = viscosity[0] * coupling[0] + viscosity[1] * coupling[1]
    flat_coupling = jnp.transpose(coupling, (0, 2, 1)).reshape(MODES * MODES, MODES)
    mixing_rows = jnp.transpose(mixing)

    both = jnp.stack([velocity, vorticity], axis=0).reshape(
        2, row_count, 3, slab_rows, group_count, chunk
    )
    main = jnp.transpose(both, (4, 0, 2, 1, 3, 5)).reshape(group_count, -1)
    left = jnp.roll(both[..., chunk - 1], 1, axis=4)
    right = jnp.roll(both[..., 0], -1, axis=4)
    rims = jnp.stack([left, right], axis=-1)
    rims = jnp.transpose(rims, (4, 0, 2, 1, 3, 5)).reshape(group_count, -1)
    main_len = main.shape[1]
    sent = jnp.concatenate([main, rims], axis=1).reshape(group_count, -1, 128)
    arrived = lax.all_to_all(sent, "mode", split_axis=0, concat_axis=0, tiled=True)
    arrived = arrived.reshape(group_count, -1)
    body = arrived[:, :main_len].reshape(MODES, halves, 2, 3, row_count, piece)
    body = jnp.transpose(body, (2, 3, 0, 1, 4, 5)).reshape(2, 3, MODES, planes, piece)
    edge = arrived[:, main_len:].reshape(MODES, halves, 2, 3, row_count, slab_rows, 2)
    edge = jnp.transpose(edge, (2, 3, 0, 1, 4, 5, 6)).reshape(2, 3, MODES, planes, slab_rows, 2)

    def coupled(speed, spin):
        shape = spin.shape
        mixed = [
            jnp.dot(flat_coupling, spin[c].reshape(MODES, -1), precision=lax.Precision.HIGHEST)
            .reshape((MODES, MODES) + shape[2:])
            for c in range(3)
        ]
        flux = [
            jnp.sum(speed[1][:, None] * mixed[2] - speed[2][:, None] * mixed[1], axis=0),
            jnp.sum(speed[2][:, None] * mixed[0] - speed[0][:, None] * mixed[2], axis=0),
            jnp.sum(speed[0][:, None] * mixed[1] - speed[1][:, None] * mixed[0], axis=0),
        ]
        damped = [
            jnp.dot(mixing_rows, spin[c].reshape(MODES, -1), precision=lax.Precision.HIGHEST)
            .reshape((MODES,) + shape[2:])
            for c in range(3)
        ]
        return flux, damped

    flux, damped = coupled(body[0], body[1])
    flux_rim, damped_rim = coupled(edge[0], edge[1])

    count = lax.axis_size("tile")
    forward = [(i, (i + 1) % count) for i in range(count)]
    backward = [((i + 1) % count, i) for i in range(count)]
    x_needs = jnp.stack([flux[1], flux[2], damped[0], damped[1], damped[2]], axis=0)
    x_shape = x_needs[..., :chunk].shape
    low = lax.ppermute(x_needs[..., piece - chunk :].reshape(-1, 128), "tile", forward)
    high = lax.ppermute(x_needs[..., :chunk].reshape(-1, 128), "tile", backward)
    low = low.reshape(x_shape)
    high = high.reshape(x_shape)

    fields = jnp.stack(flux + damped, axis=0)
    rims = jnp.stack(flux_rim + damped_rim, axis=0)
    rims = jnp.transpose(rims, (0, 1, 4, 3, 2))[..., None]
    low = jnp.tile(low, (1, 1, 1, slab_rows))
    high = jnp.tile(high, (1, 1, 1, slab_rows))
    rate = pl.pallas_call(
        functools.partial(stencil_kernel, chunk, slab_rows),
        out_shape=jax.ShapeDtypeStruct((MODES, 3, planes, piece), jnp.float32),
        in_specs=[pl.BlockSpec(memory_space=pltpu.VMEM)] * 4,
        out_specs=pl.BlockSpec(memory_space=pltpu.VMEM),
        cost_estimate=pl.CostEstimate(
            flops=MODES * 3 * planes * piece * 40,
            bytes_accessed=(6 + 10 + 3) * MODES * planes * piece * 4,
            transcendentals=0,
        ),
    )(fields, rims, low, high)
    rate = rate.reshape(MODES, 3, halves, row_count, piece)
    rate = jnp.transpose(rate, (0, 2, 1, 3, 4)).reshape(group_count, -1, 128)
    returned = lax.all_to_all(rate, "mode", split_axis=0, concat_axis=0, tiled=True)
    returned = returned.reshape(group_count, 3, row_count, slab_rows, chunk)
    returned = jnp.transpose(returned, (2, 1, 3, 0, 4))
    return returned.reshape(row_count, 3, cell_count)


def solution(mesh):
    in_specs = (P("mode", None, "tile"), P("mode", None, "tile"), P())
    out_specs = P("mode", None, "tile")
    return jax.shard_map(shards, mesh=mesh, in_specs=in_specs, out_specs=out_specs, check_vma=False)
```

```python
import functools
import math

import jax
import jax.numpy as jnp
import numpy as np
from jax import lax
from jax.experimental import pallas as pl
from jax.experimental.pallas import tpu as pltpu
from jax.sharding import PartitionSpec as P

MODES = 8
NY = 1024


def padded(block, sides, width):
    for axis, dim in sides:
        count = lax.axis_size(axis)
        forward = [(i, i + 1) for i in range(count - 1)]
        forward.append((count - 1, 0))
        backward = [(target, source) for source, target in forward]
        low = lax.ppermute(
            lax.slice_in_dim(block, block.shape[dim] - width, None, axis=dim), axis, forward
        )
        high = lax.ppermute(lax.slice_in_dim(block, 0, width, axis=dim), axis, backward)
        block = jnp.concatenate([low, block, high], axis=dim)
    return block


def legendre_list(count, where):
    values_list = [1.0, where]
    for degree in range(1, count):
        values_list.append(
            ((2 * degree + 1) * where * values_list[degree] - degree * values_list[degree - 1])
            / (degree + 1)
        )
    return values_list


def gauss_nodes(order):
    nodes_list = []
    weights_list = []
    for number in range(order):
        guess = math.cos(math.pi * (number + 0.75) / (order + 0.5))
        for sweep in range(60):
            values_list = legendre_list(order, guess)
            slope = (
                order
                * (guess * values_list[order] - values_list[order - 1])
                / (guess * guess - 1.0)
            )
            guess = guess - values_list[order] / slope
        values_list = legendre_list(order, guess)
        slope = (
            order * (guess * values_list[order] - values_list[order - 1]) / (guess * guess - 1.0)
        )
        nodes_list.append(guess)
        weights_list.append(2.0 / ((1.0 - guess * guess) * slope * slope))
    return (nodes_list, weights_list)


def triple_table(mode_count):
    nodes_list, weights_list = gauss_nodes(2 * mode_count)
    scaled = [
        [
            math.sqrt(2.0 * degree + 1.0) * legendre_list(mode_count, node_value)[degree]
            for degree in range(mode_count)
        ]
        for node_value in nodes_list
    ]
    table = [
        [
            [
                0.5
                * sum(
                    (
                        weights_list[number]
                        * scaled[number][first]
                        * scaled[number][second]
                        * scaled[number][third]
                        for number in range(len(nodes_list))
                    )
                )
                for third in range(mode_count)
            ]
            for second in range(mode_count)
        ]
        for first in range(mode_count)
    ]
    return np.array(table)


def cross_along(left_vec, right_vec, direction):

    def component(vector, number):
        return lax.index_in_dim(vector, number, direction, keepdims=False)

    components = [
        component(left_vec, 1) * component(right_vec, 2)
        - component(left_vec, 2) * component(right_vec, 1),
        component(left_vec, 2) * component(right_vec, 0)
        - component(left_vec, 0) * component(right_vec, 2),
        component(left_vec, 0) * component(right_vec, 1)
        - component(left_vec, 1) * component(right_vec, 0),
    ]
    return jnp.stack(components, axis=direction)


def centred(source_field, direction):
    return 0.5 * (jnp.roll(source_field, -1, direction) - jnp.roll(source_field, 1, direction))


def second_diff(source_field, direction):
    return (
        jnp.roll(source_field, -1, direction)
        + jnp.roll(source_field, 1, direction)
        - 2.0 * source_field
    )


def stencil_kernel(chunk, slab_rows, f_ref, r_ref, h_ref, o_ref):
    planes, piece = f_ref.shape[2], f_ref.shape[3]
    lane = lax.broadcasted_iota(jnp.int32, (planes, piece), 1)
    y_of = lane % chunk
    x_of = lane // chunk
    first_y = y_of == 0
    last_y = y_of == chunk - 1
    first_x = x_of == 0
    last_x = x_of == slab_rows - 1

    for k in range(f_ref.shape[1]):

        def moved(c, halo):
            f = f_ref[c, k]
            y_up = jnp.where(last_y, r_ref[c, k], pltpu.roll(f, piece - 1, 1))
            y_down = jnp.where(first_y, r_ref[c, k], pltpu.roll(f, 1, 1))
            z_up = pltpu.roll(f, planes - 1, 0)
            z_down = pltpu.roll(f, 1, 0)
            if halo is None:
                return f, y_up, y_down, z_up, z_down, None, None
            x_up = jnp.where(last_x, h_ref[halo, k], pltpu.roll(f, piece - chunk, 1))
            x_down = jnp.where(first_x, h_ref[halo, k], pltpu.roll(f, chunk, 1))
            return f, y_up, y_down, z_up, z_down, x_up, x_down

        def laplace(c):
            f, y_up, y_down, z_up, z_down, x_up, x_down = moved(3 + c, 2 + c)
            return (z_up + z_down - 2.0 * f) + (x_up + x_down - 2.0 * f) + (y_up + y_down - 2.0 * f)

        _, fx_yu, fx_yd, fx_zu, fx_zd, _, _ = moved(0, None)
        _, fy_yu, fy_yd, fy_zu, fy_zd, fy_xu, fy_xd = moved(1, 0)
        _, fz_yu, fz_yd, fz_zu, fz_zd, fz_xu, fz_xd = moved(2, 1)
        o_ref[k, 0] = 0.5 * (fz_yu - fz_yd) - 0.5 * (fy_zu - fy_zd) + laplace(0)
        o_ref[k, 1] = 0.5 * (fx_zu - fx_zd) - 0.5 * (fz_xu - fz_xd) + laplace(1)
        o_ref[k, 2] = 0.5 * (fy_xu - fy_xd) - 0.5 * (fx_yu - fx_yd) + laplace(2)


def shards(velocity, vorticity, viscosity):
    row_count = velocity.shape[0]
    cell_count = velocity.shape[2]
    slab_rows = cell_count // NY
    group_count = lax.axis_size("mode")
    chunk = NY // group_count
    piece = slab_rows * chunk
    halves = group_count // MODES
    planes = row_count * halves
    coupling = jnp.asarray(triple_table(MODES), dtype=jnp.float32)
    mixing = viscosity[0] * coupling[0] + viscosity[1] * coupling[1]
    flat_coupling = jnp.transpose(coupling, (0, 2, 1)).reshape(MODES * MODES, MODES)
    mixing_rows = jnp.transpose(mixing)

    both = jnp.stack([velocity, vorticity], axis=0).reshape(
        2, row_count, 3, slab_rows, group_count, chunk
    )
    main = jnp.transpose(both, (4, 0, 2, 1, 3, 5)).reshape(group_count, -1, 128)
    main_len = main.shape[1] * 128
    column = np.arange(NY)
    target = np.arange(group_count) * chunk
    picks = np.stack([(target - 1) % NY, (target + chunk) % NY], axis=-1).reshape(-1)
    select = jnp.asarray((column[:, None] == picks[None, :]).astype(np.float32))
    rims = jnp.dot(both.reshape(-1, NY), select, precision=lax.Precision.HIGHEST)
    rims = rims.reshape(2, row_count, 3, slab_rows, group_count, 2)
    rims = jnp.transpose(rims, (4, 0, 2, 1, 3, 5)).reshape(group_count, -1, 128)
    sent = jnp.concatenate([main, rims], axis=1)
    arrived = lax.all_to_all(sent, "mode", split_axis=0, concat_axis=0, tiled=True)
    arrived = arrived.reshape(group_count, -1)
    body = arrived[:, :main_len].reshape(MODES, halves, 2, 3, row_count, piece)
    body = jnp.transpose(body, (2, 3, 0, 1, 4, 5)).reshape(2, 3, MODES, planes, piece)
    edge = arrived[:, main_len:].reshape(MODES, halves, 2, 3, row_count, slab_rows, 2)
    edge = jnp.transpose(edge, (2, 3, 0, 1, 4, 5, 6)).reshape(2, 3, MODES, planes, slab_rows, 2)

    def coupled(speed, spin):
        shape = spin.shape
        mixed = [
            jnp.dot(flat_coupling, spin[c].reshape(MODES, -1), precision=lax.Precision.HIGHEST)
            .reshape((MODES, MODES) + shape[2:])
            for c in range(3)
        ]
        flux = [
            jnp.sum(speed[1][:, None] * mixed[2] - speed[2][:, None] * mixed[1], axis=0),
            jnp.sum(speed[2][:, None] * mixed[0] - speed[0][:, None] * mixed[2], axis=0),
            jnp.sum(speed[0][:, None] * mixed[1] - speed[1][:, None] * mixed[0], axis=0),
        ]
        damped = [
            jnp.dot(mixing_rows, spin[c].reshape(MODES, -1), precision=lax.Precision.HIGHEST)
            .reshape((MODES,) + shape[2:])
            for c in range(3)
        ]
        return flux, damped

    flux, damped = coupled(body[0], body[1])
    flux_rim, damped_rim = coupled(edge[0], edge[1])

    count = lax.axis_size("tile")
    forward = [(i, (i + 1) % count) for i in range(count)]
    backward = [((i + 1) % count, i) for i in range(count)]
    x_needs = jnp.stack([flux[1], flux[2], damped[0], damped[1], damped[2]], axis=0)
    x_shape = x_needs[..., :chunk].shape
    low = lax.ppermute(x_needs[..., piece - chunk :].reshape(-1, 128), "tile", forward)
    high = lax.ppermute(x_needs[..., :chunk].reshape(-1, 128), "tile", backward)
    low = low.reshape(x_shape)
    high = high.reshape(x_shape)

    fields = jnp.stack(flux + damped, axis=0)
    rims = jnp.stack(flux_rim + damped_rim, axis=0).reshape(-1, slab_rows * 2)
    lane = np.arange(piece)
    slot = (lane // chunk) * 2 + (lane % chunk == chunk - 1)
    edge_lane = (lane % chunk == 0) | (lane % chunk == chunk - 1)
    place = (np.arange(slab_rows * 2)[:, None] == slot[None, :]) & edge_lane[None, :]
    rims = jnp.dot(rims, jnp.asarray(place.astype(np.float32)), precision=lax.Precision.HIGHEST)
    rims = rims.reshape(fields.shape)
    width = piece - chunk
    halo = jnp.pad(low, ((0, 0), (0, 0), (0, 0), (0, width))) + jnp.pad(
        high, ((0, 0), (0, 0), (0, 0), (width, 0))
    )
    rate = pl.pallas_call(
        functools.partial(stencil_kernel, chunk, slab_rows),
        out_shape=jax.ShapeDtypeStruct((MODES, 3, planes, piece), jnp.float32),
        in_specs=[pl.BlockSpec(memory_space=pltpu.VMEM)] * 3,
        out_specs=pl.BlockSpec(memory_space=pltpu.VMEM),
        cost_estimate=pl.CostEstimate(
            flops=MODES * 3 * planes * piece * 40,
            bytes_accessed=(6 + 6 + 5 + 3) * MODES * planes * piece * 4,
            transcendentals=0,
        ),
    )(fields, rims, halo)
    rate = rate.reshape(MODES, 3, halves, row_count, piece)
    rate = jnp.transpose(rate, (0, 2, 1, 3, 4)).reshape(group_count, -1, 128)
    returned = lax.all_to_all(rate, "mode", split_axis=0, concat_axis=0, tiled=True)
    returned = returned.reshape(group_count, 3, row_count, slab_rows, chunk)
    returned = jnp.transpose(returned, (2, 1, 3, 0, 4))
    return returned.reshape(row_count, 3, cell_count)


def solution(mesh):
    in_specs = (P("mode", None, "tile"), P("mode", None, "tile"), P())
    out_specs = P("mode", None, "tile")
    return jax.shard_map(shards, mesh=mesh, in_specs=in_specs, out_specs=out_specs, check_vma=False)
```

```python
import functools
import math

import jax
import jax.numpy as jnp
import numpy as np
from jax import lax
from jax.experimental import pallas as pl
from jax.experimental.pallas import tpu as pltpu
from jax.sharding import PartitionSpec as P

MODES = 8
NY = 1024


def padded(block, sides, width):
    for axis, dim in sides:
        count = lax.axis_size(axis)
        forward = [(i, i + 1) for i in range(count - 1)]
        forward.append((count - 1, 0))
        backward = [(target, source) for source, target in forward]
        low = lax.ppermute(
            lax.slice_in_dim(block, block.shape[dim] - width, None, axis=dim), axis, forward
        )
        high = lax.ppermute(lax.slice_in_dim(block, 0, width, axis=dim), axis, backward)
        block = jnp.concatenate([low, block, high], axis=dim)
    return block


def legendre_list(count, where):
    values_list = [1.0, where]
    for degree in range(1, count):
        values_list.append(
            ((2 * degree + 1) * where * values_list[degree] - degree * values_list[degree - 1])
            / (degree + 1)
        )
    return values_list


def gauss_nodes(order):
    nodes_list = []
    weights_list = []
    for number in range(order):
        guess = math.cos(math.pi * (number + 0.75) / (order + 0.5))
        for sweep in range(60):
            values_list = legendre_list(order, guess)
            slope = (
                order
                * (guess * values_list[order] - values_list[order - 1])
                / (guess * guess - 1.0)
            )
            guess = guess - values_list[order] / slope
        values_list = legendre_list(order, guess)
        slope = (
            order * (guess * values_list[order] - values_list[order - 1]) / (guess * guess - 1.0)
        )
        nodes_list.append(guess)
        weights_list.append(2.0 / ((1.0 - guess * guess) * slope * slope))
    return (nodes_list, weights_list)


def triple_table(mode_count):
    nodes_list, weights_list = gauss_nodes(2 * mode_count)
    scaled = [
        [
            math.sqrt(2.0 * degree + 1.0) * legendre_list(mode_count, node_value)[degree]
            for degree in range(mode_count)
        ]
        for node_value in nodes_list
    ]
    table = [
        [
            [
                0.5
                * sum(
                    (
                        weights_list[number]
                        * scaled[number][first]
                        * scaled[number][second]
                        * scaled[number][third]
                        for number in range(len(nodes_list))
                    )
                )
                for third in range(mode_count)
            ]
            for second in range(mode_count)
        ]
        for first in range(mode_count)
    ]
    return np.array(table)


def cross_along(left_vec, right_vec, direction):

    def component(vector, number):
        return lax.index_in_dim(vector, number, direction, keepdims=False)

    components = [
        component(left_vec, 1) * component(right_vec, 2)
        - component(left_vec, 2) * component(right_vec, 1),
        component(left_vec, 2) * component(right_vec, 0)
        - component(left_vec, 0) * component(right_vec, 2),
        component(left_vec, 0) * component(right_vec, 1)
        - component(left_vec, 1) * component(right_vec, 0),
    ]
    return jnp.stack(components, axis=direction)


def centred(source_field, direction):
    return 0.5 * (jnp.roll(source_field, -1, direction) - jnp.roll(source_field, 1, direction))


def second_diff(source_field, direction):
    return (
        jnp.roll(source_field, -1, direction)
        + jnp.roll(source_field, 1, direction)
        - 2.0 * source_field
    )


def stencil_kernel(chunk, slab_rows, f_ref, r_ref, h_ref, o_ref):
    planes, piece = f_ref.shape[2], f_ref.shape[3]
    lane = lax.broadcasted_iota(jnp.int32, (planes, piece), 1)
    y_of = lane % chunk
    x_of = lane // chunk
    first_y = y_of == 0
    last_y = y_of == chunk - 1
    first_x = x_of == 0
    last_x = x_of == slab_rows - 1

    for k in range(f_ref.shape[1]):

        def moved(c, halo):
            f = f_ref[c, k]
            y_up = jnp.where(last_y, r_ref[c, k], pltpu.roll(f, piece - 1, 1))
            y_down = jnp.where(first_y, r_ref[c, k], pltpu.roll(f, 1, 1))
            z_up = pltpu.roll(f, planes - 1, 0)
            z_down = pltpu.roll(f, 1, 0)
            if halo is None:
                return f, y_up, y_down, z_up, z_down, None, None
            x_up = jnp.where(last_x, h_ref[halo, k], pltpu.roll(f, piece - chunk, 1))
            x_down = jnp.where(first_x, h_ref[halo, k], pltpu.roll(f, chunk, 1))
            return f, y_up, y_down, z_up, z_down, x_up, x_down

        def laplace(c):
            f, y_up, y_down, z_up, z_down, x_up, x_down = moved(3 + c, 2 + c)
            return (z_up + z_down - 2.0 * f) + (x_up + x_down - 2.0 * f) + (y_up + y_down - 2.0 * f)

        _, fx_yu, fx_yd, fx_zu, fx_zd, _, _ = moved(0, None)
        _, fy_yu, fy_yd, fy_zu, fy_zd, fy_xu, fy_xd = moved(1, 0)
        _, fz_yu, fz_yd, fz_zu, fz_zd, fz_xu, fz_xd = moved(2, 1)
        o_ref[k, 0] = 0.5 * (fz_yu - fz_yd) - 0.5 * (fy_zu - fy_zd) + laplace(0)
        o_ref[k, 1] = 0.5 * (fx_zu - fx_zd) - 0.5 * (fz_xu - fz_xd) + laplace(1)
        o_ref[k, 2] = 0.5 * (fy_xu - fy_xd) - 0.5 * (fx_yu - fx_yd) + laplace(2)


def shards(velocity, vorticity, viscosity):
    row_count = velocity.shape[0]
    cell_count = velocity.shape[2]
    slab_rows = cell_count // NY
    group_count = lax.axis_size("mode")
    chunk = NY // group_count
    piece = slab_rows * chunk
    halves = group_count // MODES
    planes = row_count * halves
    coupling = jnp.asarray(triple_table(MODES), dtype=jnp.float32)
    mixing = viscosity[0] * coupling[0] + viscosity[1] * coupling[1]
    flat_coupling = jnp.transpose(coupling, (0, 2, 1)).reshape(MODES * MODES, MODES)
    mixing_rows = jnp.transpose(mixing)

    both = jnp.stack([velocity, vorticity], axis=0).reshape(
        2, row_count, 3, slab_rows, group_count, chunk
    )
    main = jnp.transpose(both, (4, 0, 2, 1, 3, 5)).reshape(group_count, -1, 128)
    main_len = main.shape[1] * 128
    column = np.arange(NY)
    target = np.arange(group_count) * chunk
    picks = np.stack([(target - 1) % NY, (target + chunk) % NY], axis=-1).reshape(-1)
    select = jnp.asarray((column[:, None] == picks[None, :]).astype(np.float32))
    rims = jnp.dot(both.reshape(-1, NY), select, precision=lax.Precision.HIGHEST)
    rims = rims.reshape(2, row_count, 3, slab_rows, group_count, 2)
    rims = jnp.transpose(rims, (4, 0, 2, 1, 3, 5)).reshape(group_count, -1, 128)
    sent = jnp.concatenate([main, rims], axis=1)
    arrived = lax.all_to_all(sent, "mode", split_axis=0, concat_axis=0, tiled=True)
    arrived = arrived.reshape(group_count, -1)
    body = arrived[:, :main_len].reshape(MODES, halves, 2, 3, row_count, piece)
    body = jnp.transpose(body, (2, 3, 0, 1, 4, 5)).reshape(2, 3, MODES, planes, piece)
    edge = arrived[:, main_len:].reshape(MODES, halves, 2, 3, row_count * slab_rows * 2)
    edge = jnp.transpose(edge, (2, 3, 0, 1, 4)).reshape(2, 3, MODES, planes * slab_rows * 2)

    def coupled(speed, spin):
        shape = spin.shape
        mixed = [
            jnp.dot(flat_coupling, spin[c].reshape(MODES, -1), precision=lax.Precision.HIGHEST)
            .reshape((MODES, MODES) + shape[2:])
            for c in range(3)
        ]
        flux = [
            jnp.sum(speed[1][:, None] * mixed[2] - speed[2][:, None] * mixed[1], axis=0),
            jnp.sum(speed[2][:, None] * mixed[0] - speed[0][:, None] * mixed[2], axis=0),
            jnp.sum(speed[0][:, None] * mixed[1] - speed[1][:, None] * mixed[0], axis=0),
        ]
        damped = [
            jnp.dot(mixing_rows, spin[c].reshape(MODES, -1), precision=lax.Precision.HIGHEST)
            .reshape((MODES,) + shape[2:])
            for c in range(3)
        ]
        return flux, damped

    flux, damped = coupled(body[0], body[1])
    flux_rim, damped_rim = coupled(edge[0], edge[1])

    count = lax.axis_size("tile")
    forward = [(i, (i + 1) % count) for i in range(count)]
    backward = [((i + 1) % count, i) for i in range(count)]
    x_needs = jnp.stack([flux[1], flux[2], damped[0], damped[1], damped[2]], axis=0)
    x_shape = x_needs[..., :chunk].shape
    low = lax.ppermute(x_needs[..., piece - chunk :].reshape(-1, 128), "tile", forward)
    high = lax.ppermute(x_needs[..., :chunk].reshape(-1, 128), "tile", backward)
    low = low.reshape(x_shape)
    high = high.reshape(x_shape)

    fields = jnp.stack(flux + damped, axis=0)
    rims = jnp.stack(flux_rim + damped_rim, axis=0).reshape(-1, slab_rows * 2)
    lane = np.arange(piece)
    slot = (lane // chunk) * 2 + (lane % chunk == chunk - 1)
    edge_lane = (lane % chunk == 0) | (lane % chunk == chunk - 1)
    place = (np.arange(slab_rows * 2)[:, None] == slot[None, :]) & edge_lane[None, :]
    rims = jnp.dot(rims, jnp.asarray(place.astype(np.float32)), precision=lax.Precision.HIGHEST)
    rims = rims.reshape(fields.shape)
    width = piece - chunk
    halo = jnp.pad(low, ((0, 0), (0, 0), (0, 0), (0, width))) + jnp.pad(
        high, ((0, 0), (0, 0), (0, 0), (width, 0))
    )
    rate = pl.pallas_call(
        functools.partial(stencil_kernel, chunk, slab_rows),
        out_shape=jax.ShapeDtypeStruct((MODES, 3, planes, piece), jnp.float32),
        in_specs=[pl.BlockSpec(memory_space=pltpu.VMEM)] * 3,
        out_specs=pl.BlockSpec(memory_space=pltpu.VMEM),
        cost_estimate=pl.CostEstimate(
            flops=MODES * 3 * planes * piece * 40,
            bytes_accessed=(6 + 6 + 5 + 3) * MODES * planes * piece * 4,
            transcendentals=0,
        ),
    )(fields, rims, halo)
    rate = rate.reshape(MODES, 3, halves, row_count, piece)
    rate = jnp.transpose(rate, (0, 2, 1, 3, 4)).reshape(group_count, -1, 128)
    returned = lax.all_to_all(rate, "mode", split_axis=0, concat_axis=0, tiled=True)
    returned = returned.reshape(group_count, 3, row_count, slab_rows, chunk)
    returned = jnp.transpose(returned, (2, 1, 3, 0, 4))
    return returned.reshape(row_count, 3, cell_count)


def solution(mesh):
    in_specs = (P("mode", None, "tile"), P("mode", None, "tile"), P())
    out_specs = P("mode", None, "tile")
    return jax.shard_map(shards, mesh=mesh, in_specs=in_specs, out_specs=out_specs, check_vma=False)
```

```python
import functools
import math

import jax
import jax.numpy as jnp
import numpy as np
from jax import lax
from jax.experimental import pallas as pl
from jax.experimental.pallas import tpu as pltpu
from jax.sharding import PartitionSpec as P

MODES = 8
NY = 1024


def padded(block, sides, width):
    for axis, dim in sides:
        count = lax.axis_size(axis)
        forward = [(i, i + 1) for i in range(count - 1)]
        forward.append((count - 1, 0))
        backward = [(target, source) for source, target in forward]
        low = lax.ppermute(
            lax.slice_in_dim(block, block.shape[dim] - width, None, axis=dim), axis, forward
        )
        high = lax.ppermute(lax.slice_in_dim(block, 0, width, axis=dim), axis, backward)
        block = jnp.concatenate([low, block, high], axis=dim)
    return block


def legendre_list(count, where):
    values_list = [1.0, where]
    for degree in range(1, count):
        values_list.append(
            ((2 * degree + 1) * where * values_list[degree] - degree * values_list[degree - 1])
            / (degree + 1)
        )
    return values_list


def gauss_nodes(order):
    nodes_list = []
    weights_list = []
    for number in range(order):
        guess = math.cos(math.pi * (number + 0.75) / (order + 0.5))
        for sweep in range(60):
            values_list = legendre_list(order, guess)
            slope = (
                order
                * (guess * values_list[order] - values_list[order - 1])
                / (guess * guess - 1.0)
            )
            guess = guess - values_list[order] / slope
        values_list = legendre_list(order, guess)
        slope = (
            order * (guess * values_list[order] - values_list[order - 1]) / (guess * guess - 1.0)
        )
        nodes_list.append(guess)
        weights_list.append(2.0 / ((1.0 - guess * guess) * slope * slope))
    return (nodes_list, weights_list)


def triple_table(mode_count):
    nodes_list, weights_list = gauss_nodes(2 * mode_count)
    scaled = [
        [
            math.sqrt(2.0 * degree + 1.0) * legendre_list(mode_count, node_value)[degree]
            for degree in range(mode_count)
        ]
        for node_value in nodes_list
    ]
    table = [
        [
            [
                0.5
                * sum(
                    (
                        weights_list[number]
                        * scaled[number][first]
                        * scaled[number][second]
                        * scaled[number][third]
                        for number in range(len(nodes_list))
                    )
                )
                for third in range(mode_count)
            ]
            for second in range(mode_count)
        ]
        for first in range(mode_count)
    ]
    return np.array(table)


def cross_along(left_vec, right_vec, direction):

    def component(vector, number):
        return lax.index_in_dim(vector, number, direction, keepdims=False)

    components = [
        component(left_vec, 1) * component(right_vec, 2)
        - component(left_vec, 2) * component(right_vec, 1),
        component(left_vec, 2) * component(right_vec, 0)
        - component(left_vec, 0) * component(right_vec, 2),
        component(left_vec, 0) * component(right_vec, 1)
        - component(left_vec, 1) * component(right_vec, 0),
    ]
    return jnp.stack(components, axis=direction)


def centred(source_field, direction):
    return 0.5 * (jnp.roll(source_field, -1, direction) - jnp.roll(source_field, 1, direction))


def second_diff(source_field, direction):
    return (
        jnp.roll(source_field, -1, direction)
        + jnp.roll(source_field, 1, direction)
        - 2.0 * source_field
    )


def stencil_kernel(chunk, slab_rows, f_ref, r_ref, h_ref, o_ref):
    planes, piece = f_ref.shape[2], f_ref.shape[3]
    lane = lax.broadcasted_iota(jnp.int32, (planes, piece), 1)
    y_of = lane % chunk
    x_of = lane // chunk
    first_y = y_of == 0
    last_y = y_of == chunk - 1
    first_x = x_of == 0
    last_x = x_of == slab_rows - 1

    for k in range(f_ref.shape[1]):

        def moved(c, halo):
            f = f_ref[c, k]
            y_up = jnp.where(last_y, r_ref[c, k], pltpu.roll(f, piece - 1, 1))
            y_down = jnp.where(first_y, r_ref[c, k], pltpu.roll(f, 1, 1))
            z_up = pltpu.roll(f, planes - 1, 0)
            z_down = pltpu.roll(f, 1, 0)
            if halo is None:
                return f, y_up, y_down, z_up, z_down, None, None
            x_up = jnp.where(last_x, h_ref[halo, k], pltpu.roll(f, piece - chunk, 1))
            x_down = jnp.where(first_x, h_ref[halo, k], pltpu.roll(f, chunk, 1))
            return f, y_up, y_down, z_up, z_down, x_up, x_down

        def laplace(c):
            f, y_up, y_down, z_up, z_down, x_up, x_down = moved(3 + c, 2 + c)
            return (z_up + z_down - 2.0 * f) + (x_up + x_down - 2.0 * f) + (y_up + y_down - 2.0 * f)

        _, fx_yu, fx_yd, fx_zu, fx_zd, _, _ = moved(0, None)
        _, fy_yu, fy_yd, fy_zu, fy_zd, fy_xu, fy_xd = moved(1, 0)
        _, fz_yu, fz_yd, fz_zu, fz_zd, fz_xu, fz_xd = moved(2, 1)
        o_ref[k, 0] = 0.5 * (fz_yu - fz_yd) - 0.5 * (fy_zu - fy_zd) + laplace(0)
        o_ref[k, 1] = 0.5 * (fx_zu - fx_zd) - 0.5 * (fz_xu - fz_xd) + laplace(1)
        o_ref[k, 2] = 0.5 * (fy_xu - fy_xd) - 0.5 * (fx_yu - fx_yd) + laplace(2)


def shards(velocity, vorticity, viscosity):
    row_count = velocity.shape[0]
    cell_count = velocity.shape[2]
    slab_rows = cell_count // NY
    group_count = lax.axis_size("mode")
    chunk = NY // group_count
    piece = slab_rows * chunk
    halves = group_count // MODES
    planes = row_count * halves
    coupling = jnp.asarray(triple_table(MODES), dtype=jnp.float32)
    mixing = viscosity[0] * coupling[0] + viscosity[1] * coupling[1]
    flat_coupling = jnp.transpose(coupling, (0, 2, 1)).reshape(MODES * MODES, MODES)
    mixing_rows = jnp.transpose(mixing)

    both = jnp.stack([velocity, vorticity], axis=0).reshape(
        2, row_count, 3, slab_rows, group_count, chunk
    )
    main = jnp.transpose(both, (4, 0, 2, 1, 3, 5)).reshape(group_count, -1, 128)
    main_len = main.shape[1] * 128
    column = np.arange(NY)
    target = np.arange(group_count) * chunk
    picks = np.stack([(target - 1) % NY, (target + chunk) % NY], axis=-1).reshape(-1)
    select = jnp.asarray((column[:, None] == picks[None, :]).astype(np.float32))
    rims = jnp.dot(both.reshape(-1, NY), select, precision=lax.Precision.HIGHEST)
    rims = rims.reshape(2, row_count, 3, slab_rows, group_count, 2)
    rims = jnp.transpose(rims, (4, 0, 2, 1, 3, 5)).reshape(group_count, -1, 128)
    sent = jnp.concatenate([main, rims], axis=1)
    arrived = lax.all_to_all(sent, "mode", split_axis=0, concat_axis=0, tiled=True)
    arrived = arrived.reshape(group_count, -1)
    body = arrived[:, :main_len].reshape(MODES, halves, 2, 3, row_count, piece)
    body = jnp.transpose(body, (2, 3, 0, 1, 4, 5)).reshape(2, 3, MODES, planes, piece)
    edge = arrived[:, main_len:].reshape(MODES, halves, 2, 3, row_count * slab_rows * 2)
    edge = jnp.transpose(edge, (2, 3, 0, 1, 4)).reshape(2, 3, MODES, planes * slab_rows * 2)

    def coupled(speed, spin):
        shape = spin.shape
        mixed = [
            jnp.dot(flat_coupling, spin[c].reshape(MODES, -1), precision=lax.Precision.HIGHEST)
            .reshape((MODES, MODES) + shape[2:])
            for c in range(3)
        ]
        flux = [
            jnp.sum(speed[1][:, None] * mixed[2] - speed[2][:, None] * mixed[1], axis=0),
            jnp.sum(speed[2][:, None] * mixed[0] - speed[0][:, None] * mixed[2], axis=0),
            jnp.sum(speed[0][:, None] * mixed[1] - speed[1][:, None] * mixed[0], axis=0),
        ]
        damped = [
            jnp.dot(mixing_rows, spin[c].reshape(MODES, -1), precision=lax.Precision.HIGHEST)
            .reshape((MODES,) + shape[2:])
            for c in range(3)
        ]
        return flux, damped

    flux, damped = coupled(body[0], body[1])
    flux_rim, damped_rim = coupled(edge[0], edge[1])

    count = lax.axis_size("tile")
    forward = [(i, (i + 1) % count) for i in range(count)]
    backward = [((i + 1) % count, i) for i in range(count)]
    x_needs = jnp.stack([flux[1], flux[2], damped[0], damped[1], damped[2]], axis=0)
    x_shape = x_needs[..., :chunk].shape
    low = lax.ppermute(x_needs[..., piece - chunk :].reshape(-1, 128), "tile", forward)
    high = lax.ppermute(x_needs[..., :chunk].reshape(-1, 128), "tile", backward)
    low = low.reshape(x_shape)
    high = high.reshape(x_shape)

    fields = jnp.stack(flux + damped, axis=0)
    rims = lax.optimization_barrier(jnp.stack(flux_rim + damped_rim, axis=0))
    rims = rims.reshape(6, MODES, planes, slab_rows * 2)
    lane = lax.broadcasted_iota(jnp.int32, (1, 1, 1, piece), 3)
    slot = (lane // chunk) * 2 + (lane % chunk == chunk - 1).astype(jnp.int32)
    edge_lane = (lane % chunk == 0) | (lane % chunk == chunk - 1)
    placed = jnp.zeros(fields.shape, jnp.float32)
    for number in range(slab_rows * 2):
        placed = jnp.where(edge_lane & (slot == number), rims[..., number : number + 1], placed)
    rims = placed
    width = piece - chunk
    halo = jnp.pad(low, ((0, 0), (0, 0), (0, 0), (0, width))) + jnp.pad(
        high, ((0, 0), (0, 0), (0, 0), (width, 0))
    )
    rate = pl.pallas_call(
        functools.partial(stencil_kernel, chunk, slab_rows),
        out_shape=jax.ShapeDtypeStruct((MODES, 3, planes, piece), jnp.float32),
        in_specs=[pl.BlockSpec(memory_space=pltpu.VMEM)] * 3,
        out_specs=pl.BlockSpec(memory_space=pltpu.VMEM),
        cost_estimate=pl.CostEstimate(
            flops=MODES * 3 * planes * piece * 40,
            bytes_accessed=(6 + 6 + 5 + 3) * MODES * planes * piece * 4,
            transcendentals=0,
        ),
    )(fields, rims, halo)
    rate = rate.reshape(MODES, 3, halves, row_count, piece)
    rate = jnp.transpose(rate, (0, 2, 1, 3, 4)).reshape(group_count, -1, 128)
    returned = lax.all_to_all(rate, "mode", split_axis=0, concat_axis=0, tiled=True)
    returned = returned.reshape(group_count, 3, row_count, slab_rows, chunk)
    returned = jnp.transpose(returned, (2, 1, 3, 0, 4))
    return returned.reshape(row_count, 3, cell_count)


def solution(mesh):
    in_specs = (P("mode", None, "tile"), P("mode", None, "tile"), P())
    out_specs = P("mode", None, "tile")
    return jax.shard_map(shards, mesh=mesh, in_specs=in_specs, out_specs=out_specs, check_vma=False)
```

```python
import functools
import math

import jax
import jax.numpy as jnp
import numpy as np
from jax import lax
from jax.experimental import pallas as pl
from jax.experimental.pallas import tpu as pltpu
from jax.sharding import PartitionSpec as P

MODES = 8
NY = 1024


def padded(block, sides, width):
    for axis, dim in sides:
        count = lax.axis_size(axis)
        forward = [(i, i + 1) for i in range(count - 1)]
        forward.append((count - 1, 0))
        backward = [(target, source) for source, target in forward]
        low = lax.ppermute(
            lax.slice_in_dim(block, block.shape[dim] - width, None, axis=dim), axis, forward
        )
        high = lax.ppermute(lax.slice_in_dim(block, 0, width, axis=dim), axis, backward)
        block = jnp.concatenate([low, block, high], axis=dim)
    return block


def legendre_list(count, where):
    values_list = [1.0, where]
    for degree in range(1, count):
        values_list.append(
            ((2 * degree + 1) * where * values_list[degree] - degree * values_list[degree - 1])
            / (degree + 1)
        )
    return values_list


def gauss_nodes(order):
    nodes_list = []
    weights_list = []
    for number in range(order):
        guess = math.cos(math.pi * (number + 0.75) / (order + 0.5))
        for sweep in range(60):
            values_list = legendre_list(order, guess)
            slope = (
                order
                * (guess * values_list[order] - values_list[order - 1])
                / (guess * guess - 1.0)
            )
            guess = guess - values_list[order] / slope
        values_list = legendre_list(order, guess)
        slope = (
            order * (guess * values_list[order] - values_list[order - 1]) / (guess * guess - 1.0)
        )
        nodes_list.append(guess)
        weights_list.append(2.0 / ((1.0 - guess * guess) * slope * slope))
    return (nodes_list, weights_list)


def triple_table(mode_count):
    nodes_list, weights_list = gauss_nodes(2 * mode_count)
    scaled = [
        [
            math.sqrt(2.0 * degree + 1.0) * legendre_list(mode_count, node_value)[degree]
            for degree in range(mode_count)
        ]
        for node_value in nodes_list
    ]
    table = [
        [
            [
                0.5
                * sum(
                    (
                        weights_list[number]
                        * scaled[number][first]
                        * scaled[number][second]
                        * scaled[number][third]
                        for number in range(len(nodes_list))
                    )
                )
                for third in range(mode_count)
            ]
            for second in range(mode_count)
        ]
        for first in range(mode_count)
    ]
    return np.array(table)


def cross_along(left_vec, right_vec, direction):

    def component(vector, number):
        return lax.index_in_dim(vector, number, direction, keepdims=False)

    components = [
        component(left_vec, 1) * component(right_vec, 2)
        - component(left_vec, 2) * component(right_vec, 1),
        component(left_vec, 2) * component(right_vec, 0)
        - component(left_vec, 0) * component(right_vec, 2),
        component(left_vec, 0) * component(right_vec, 1)
        - component(left_vec, 1) * component(right_vec, 0),
    ]
    return jnp.stack(components, axis=direction)


def centred(source_field, direction):
    return 0.5 * (jnp.roll(source_field, -1, direction) - jnp.roll(source_field, 1, direction))


def second_diff(source_field, direction):
    return (
        jnp.roll(source_field, -1, direction)
        + jnp.roll(source_field, 1, direction)
        - 2.0 * source_field
    )


def stencil_kernel(chunk, slab_rows, f_ref, r_ref, h_ref, o_ref):
    planes, piece = f_ref.shape[2], f_ref.shape[3]
    lane = lax.broadcasted_iota(jnp.int32, (planes, piece), 1)
    y_of = lane % chunk
    x_of = lane // chunk
    first_y = y_of == 0
    last_y = y_of == chunk - 1
    first_x = x_of == 0
    last_x = x_of == slab_rows - 1

    for k in range(f_ref.shape[1]):

        def moved(c, halo):
            f = f_ref[c, k]
            y_up = jnp.where(last_y, r_ref[c, k], pltpu.roll(f, piece - 1, 1))
            y_down = jnp.where(first_y, r_ref[c, k], pltpu.roll(f, 1, 1))
            z_up = pltpu.roll(f, planes - 1, 0)
            z_down = pltpu.roll(f, 1, 0)
            if halo is None:
                return f, y_up, y_down, z_up, z_down, None, None
            x_up = jnp.where(last_x, h_ref[halo, k], pltpu.roll(f, piece - chunk, 1))
            x_down = jnp.where(first_x, h_ref[halo, k], pltpu.roll(f, chunk, 1))
            return f, y_up, y_down, z_up, z_down, x_up, x_down

        def laplace(c):
            f, y_up, y_down, z_up, z_down, x_up, x_down = moved(3 + c, 2 + c)
            return (z_up + z_down - 2.0 * f) + (x_up + x_down - 2.0 * f) + (y_up + y_down - 2.0 * f)

        _, fx_yu, fx_yd, fx_zu, fx_zd, _, _ = moved(0, None)
        _, fy_yu, fy_yd, fy_zu, fy_zd, fy_xu, fy_xd = moved(1, 0)
        _, fz_yu, fz_yd, fz_zu, fz_zd, fz_xu, fz_xd = moved(2, 1)
        o_ref[k, 0] = 0.5 * (fz_yu - fz_yd) - 0.5 * (fy_zu - fy_zd) + laplace(0)
        o_ref[k, 1] = 0.5 * (fx_zu - fx_zd) - 0.5 * (fz_xu - fz_xd) + laplace(1)
        o_ref[k, 2] = 0.5 * (fy_xu - fy_xd) - 0.5 * (fx_yu - fx_yd) + laplace(2)


def shards(velocity, vorticity, viscosity):
    row_count = velocity.shape[0]
    cell_count = velocity.shape[2]
    slab_rows = cell_count // NY
    group_count = lax.axis_size("mode")
    chunk = NY // group_count
    piece = slab_rows * chunk
    halves = group_count // MODES
    planes = row_count * halves
    coupling = jnp.asarray(triple_table(MODES), dtype=jnp.float32)
    mixing = viscosity[0] * coupling[0] + viscosity[1] * coupling[1]
    flat_coupling = jnp.transpose(coupling, (0, 2, 1)).reshape(MODES * MODES, MODES)
    mixing_rows = jnp.transpose(mixing)

    both = jnp.stack([velocity, vorticity], axis=0).reshape(
        2, row_count, 3, slab_rows, group_count, chunk
    )
    main = jnp.transpose(both, (4, 0, 2, 1, 3, 5)).reshape(group_count, -1, 128)
    main_len = main.shape[1] * 128
    column = np.arange(NY)
    target = np.arange(group_count) * chunk
    picks = np.stack([(target - 1) % NY, (target + chunk) % NY], axis=-1).reshape(-1)
    select = jnp.asarray((column[:, None] == picks[None, :]).astype(np.float32))
    rims = jnp.dot(both.reshape(-1, NY), select, precision=lax.Precision.HIGHEST)
    rims = rims.reshape(2, row_count, 3, slab_rows, group_count, 2)
    rims = jnp.transpose(rims, (4, 0, 2, 1, 3, 5)).reshape(group_count, -1, 128)
    sent = jnp.concatenate([main, rims], axis=1)
    arrived = lax.all_to_all(sent, "mode", split_axis=0, concat_axis=0, tiled=True)
    arrived = arrived.reshape(group_count, -1)
    body = arrived[:, :main_len].reshape(MODES, halves, 2, 3, row_count, piece)
    body = jnp.transpose(body, (2, 3, 0, 1, 4, 5)).reshape(2, 3, MODES, planes, piece)
    edge = arrived[:, main_len:].reshape(MODES, halves, 2, 3, row_count * slab_rows * 2)
    edge = jnp.transpose(edge, (2, 3, 0, 1, 4)).reshape(2, 3, MODES, planes * slab_rows * 2)

    def coupled(speed, spin):
        shape = spin.shape
        mixed = [
            jnp.dot(flat_coupling, spin[c].reshape(MODES, -1), precision=lax.Precision.HIGHEST)
            .reshape((MODES, MODES) + shape[2:])
            for c in range(3)
        ]
        flux = [
            jnp.sum(speed[1][:, None] * mixed[2] - speed[2][:, None] * mixed[1], axis=0),
            jnp.sum(speed[2][:, None] * mixed[0] - speed[0][:, None] * mixed[2], axis=0),
            jnp.sum(speed[0][:, None] * mixed[1] - speed[1][:, None] * mixed[0], axis=0),
        ]
        damped = [
            jnp.dot(mixing_rows, spin[c].reshape(MODES, -1), precision=lax.Precision.HIGHEST)
            .reshape((MODES,) + shape[2:])
            for c in range(3)
        ]
        return flux, damped

    flux, damped = coupled(body[0], body[1])
    flux_rim, damped_rim = coupled(edge[0], edge[1])

    count = lax.axis_size("tile")
    forward = [(i, (i + 1) % count) for i in range(count)]
    backward = [((i + 1) % count, i) for i in range(count)]
    x_needs = jnp.stack([flux[1], flux[2], damped[0], damped[1], damped[2]], axis=0)
    x_shape = x_needs[..., :chunk].shape
    low = lax.ppermute(x_needs[..., piece - chunk :].reshape(-1, 128), "tile", forward)
    high = lax.ppermute(x_needs[..., :chunk].reshape(-1, 128), "tile", backward)
    low = low.reshape(x_shape)
    high = high.reshape(x_shape)

    fields = jnp.stack(flux + damped, axis=0)
    rims = jnp.stack(flux_rim + damped_rim, axis=0).reshape(-1, slab_rows * 2)
    lane = np.arange(piece)
    slot = (lane // chunk) * 2 + (lane % chunk == chunk - 1)
    edge_lane = (lane % chunk == 0) | (lane % chunk == chunk - 1)
    place = (np.arange(slab_rows * 2)[:, None] == slot[None, :]) & edge_lane[None, :]
    rims = jnp.dot(rims, jnp.asarray(place.astype(np.float32)), precision=lax.Precision.HIGHEST)
    rims = rims.reshape(fields.shape)
    width = piece - chunk
    halo = jnp.pad(low, ((0, 0), (0, 0), (0, 0), (0, width))) + jnp.pad(
        high, ((0, 0), (0, 0), (0, 0), (width, 0))
    )
    rate = pl.pallas_call(
        functools.partial(stencil_kernel, chunk, slab_rows),
        out_shape=jax.ShapeDtypeStruct((MODES, 3, planes, piece), jnp.float32),
        in_specs=[pl.BlockSpec(memory_space=pltpu.VMEM)] * 3,
        out_specs=pl.BlockSpec(memory_space=pltpu.VMEM),
        compiler_params=pltpu.CompilerParams(allow_input_fusion=[True, True, True]),
        cost_estimate=pl.CostEstimate(
            flops=MODES * 3 * planes * piece * 40,
            bytes_accessed=(6 + 6 + 5 + 3) * MODES * planes * piece * 4,
            transcendentals=0,
        ),
    )(fields, rims, halo)
    rate = rate.reshape(MODES, 3, halves, row_count, piece)
    rate = jnp.transpose(rate, (0, 2, 1, 3, 4)).reshape(group_count, -1, 128)
    returned = lax.all_to_all(rate, "mode", split_axis=0, concat_axis=0, tiled=True)
    returned = returned.reshape(group_count, 3, row_count, slab_rows, chunk)
    returned = jnp.transpose(returned, (2, 1, 3, 0, 4))
    return returned.reshape(row_count, 3, cell_count)


def solution(mesh):
    in_specs = (P("mode", None, "tile"), P("mode", None, "tile"), P())
    out_specs = P("mode", None, "tile")
    return jax.shard_map(shards, mesh=mesh, in_specs=in_specs, out_specs=out_specs, check_vma=False)
```

```python
import functools
import math

import jax
import jax.numpy as jnp
import numpy as np
from jax import lax
from jax.experimental import pallas as pl
from jax.experimental.pallas import tpu as pltpu
from jax.sharding import PartitionSpec as P

MODES = 8
NY = 1024


def padded(block, sides, width):
    for axis, dim in sides:
        count = lax.axis_size(axis)
        forward = [(i, i + 1) for i in range(count - 1)]
        forward.append((count - 1, 0))
        backward = [(target, source) for source, target in forward]
        low = lax.ppermute(
            lax.slice_in_dim(block, block.shape[dim] - width, None, axis=dim), axis, forward
        )
        high = lax.ppermute(lax.slice_in_dim(block, 0, width, axis=dim), axis, backward)
        block = jnp.concatenate([low, block, high], axis=dim)
    return block


def legendre_list(count, where):
    values_list = [1.0, where]
    for degree in range(1, count):
        values_list.append(
            ((2 * degree + 1) * where * values_list[degree] - degree * values_list[degree - 1])
            / (degree + 1)
        )
    return values_list


def gauss_nodes(order):
    nodes_list = []
    weights_list = []
    for number in range(order):
        guess = math.cos(math.pi * (number + 0.75) / (order + 0.5))
        for sweep in range(60):
            values_list = legendre_list(order, guess)
            slope = (
                order
                * (guess * values_list[order] - values_list[order - 1])
                / (guess * guess - 1.0)
            )
            guess = guess - values_list[order] / slope
        values_list = legendre_list(order, guess)
        slope = (
            order * (guess * values_list[order] - values_list[order - 1]) / (guess * guess - 1.0)
        )
        nodes_list.append(guess)
        weights_list.append(2.0 / ((1.0 - guess * guess) * slope * slope))
    return (nodes_list, weights_list)


def triple_table(mode_count):
    nodes_list, weights_list = gauss_nodes(2 * mode_count)
    scaled = [
        [
            math.sqrt(2.0 * degree + 1.0) * legendre_list(mode_count, node_value)[degree]
            for degree in range(mode_count)
        ]
        for node_value in nodes_list
    ]
    table = [
        [
            [
                0.5
                * sum(
                    (
                        weights_list[number]
                        * scaled[number][first]
                        * scaled[number][second]
                        * scaled[number][third]
                        for number in range(len(nodes_list))
                    )
                )
                for third in range(mode_count)
            ]
            for second in range(mode_count)
        ]
        for first in range(mode_count)
    ]
    return np.array(table)


def cross_along(left_vec, right_vec, direction):

    def component(vector, number):
        return lax.index_in_dim(vector, number, direction, keepdims=False)

    components = [
        component(left_vec, 1) * component(right_vec, 2)
        - component(left_vec, 2) * component(right_vec, 1),
        component(left_vec, 2) * component(right_vec, 0)
        - component(left_vec, 0) * component(right_vec, 2),
        component(left_vec, 0) * component(right_vec, 1)
        - component(left_vec, 1) * component(right_vec, 0),
    ]
    return jnp.stack(components, axis=direction)


def centred(source_field, direction):
    return 0.5 * (jnp.roll(source_field, -1, direction) - jnp.roll(source_field, 1, direction))


def second_diff(source_field, direction):
    return (
        jnp.roll(source_field, -1, direction)
        + jnp.roll(source_field, 1, direction)
        - 2.0 * source_field
    )


def coupling_kernel(table, visc_ref, b_ref, o_ref):
    modes = table.shape[0]
    first, second = visc_ref[0], visc_ref[1]
    mix = [
        [first * float(table[0, j, k]) + second * float(table[1, j, k]) for k in range(modes)]
        for j in range(modes)
    ]
    rows = b_ref.shape[3] // 8
    lanes = b_ref.shape[4] // 128

    def tile(number, carry):
        zs = pl.ds(pl.multiple_of((number // lanes) * 8, 8), 8)
        ls = pl.ds(pl.multiple_of((number % lanes) * 128, 128), 128)
        spin = [[b_ref[1, c, j, zs, ls] for c in range(3)] for j in range(modes)]
        for k in range(modes):
            total = [None, None, None]
            for i in range(modes):
                mixed = []
                for c in range(3):
                    acc = spin[0][c] * float(table[i, 0, k])
                    for j in range(1, modes):
                        acc = acc + spin[j][c] * float(table[i, j, k])
                    mixed.append(acc)
                speed = [b_ref[0, c, i, zs, ls] for c in range(3)]
                terms = [
                    speed[1] * mixed[2] - speed[2] * mixed[1],
                    speed[2] * mixed[0] - speed[0] * mixed[2],
                    speed[0] * mixed[1] - speed[1] * mixed[0],
                ]
                total = terms if i == 0 else [a + b for a, b in zip(total, terms)]
            for c in range(3):
                o_ref[c, k, zs, ls] = total[c]
                acc = spin[0][c] * mix[0][k]
                for j in range(1, modes):
                    acc = acc + spin[j][c] * mix[j][k]
                o_ref[3 + c, k, zs, ls] = acc
        return carry

    lax.fori_loop(0, rows * lanes, tile, 0)


def stencil_kernel(chunk, slab_rows, f_ref, r_ref, h_ref, o_ref):
    planes, piece = f_ref.shape[2], f_ref.shape[3]
    lane = lax.broadcasted_iota(jnp.int32, (planes, piece), 1)
    y_of = lane % chunk
    x_of = lane // chunk
    first_y = y_of == 0
    last_y = y_of == chunk - 1
    first_x = x_of == 0
    last_x = x_of == slab_rows - 1

    for k in range(f_ref.shape[1]):

        def moved(c, halo):
            f = f_ref[c, k]
            y_up = jnp.where(last_y, r_ref[c, k], pltpu.roll(f, piece - 1, 1))
            y_down = jnp.where(first_y, r_ref[c, k], pltpu.roll(f, 1, 1))
            z_up = pltpu.roll(f, planes - 1, 0)
            z_down = pltpu.roll(f, 1, 0)
            if halo is None:
                return f, y_up, y_down, z_up, z_down, None, None
            x_up = jnp.where(last_x, h_ref[halo, k], pltpu.roll(f, piece - chunk, 1))
            x_down = jnp.where(first_x, h_ref[halo, k], pltpu.roll(f, chunk, 1))
            return f, y_up, y_down, z_up, z_down, x_up, x_down

        def laplace(c):
            f, y_up, y_down, z_up, z_down, x_up, x_down = moved(3 + c, 2 + c)
            return (z_up + z_down - 2.0 * f) + (x_up + x_down - 2.0 * f) + (y_up + y_down - 2.0 * f)

        _, fx_yu, fx_yd, fx_zu, fx_zd, _, _ = moved(0, None)
        _, fy_yu, fy_yd, fy_zu, fy_zd, fy_xu, fy_xd = moved(1, 0)
        _, fz_yu, fz_yd, fz_zu, fz_zd, fz_xu, fz_xd = moved(2, 1)
        o_ref[k, 0] = 0.5 * (fz_yu - fz_yd) - 0.5 * (fy_zu - fy_zd) + laplace(0)
        o_ref[k, 1] = 0.5 * (fx_zu - fx_zd) - 0.5 * (fz_xu - fz_xd) + laplace(1)
        o_ref[k, 2] = 0.5 * (fy_xu - fy_xd) - 0.5 * (fx_yu - fx_yd) + laplace(2)


def shards(velocity, vorticity, viscosity):
    row_count = velocity.shape[0]
    cell_count = velocity.shape[2]
    slab_rows = cell_count // NY
    group_count = lax.axis_size("mode")
    chunk = NY // group_count
    piece = slab_rows * chunk
    halves = group_count // MODES
    planes = row_count * halves
    coupling = jnp.asarray(triple_table(MODES), dtype=jnp.float32)
    mixing = viscosity[0] * coupling[0] + viscosity[1] * coupling[1]
    flat_coupling = jnp.transpose(coupling, (0, 2, 1)).reshape(MODES * MODES, MODES)
    mixing_rows = jnp.transpose(mixing)

    both = jnp.stack([velocity, vorticity], axis=0).reshape(
        2, row_count, 3, slab_rows, group_count, chunk
    )
    main = jnp.transpose(both, (4, 0, 2, 1, 3, 5)).reshape(group_count, -1, 128)
    main_len = main.shape[1] * 128
    column = np.arange(NY)
    target = np.arange(group_count) * chunk
    picks = np.stack([(target - 1) % NY, (target + chunk) % NY], axis=-1).reshape(-1)
    select = jnp.asarray((column[:, None] == picks[None, :]).astype(np.float32))
    rims = jnp.dot(both.reshape(-1, NY), select, precision=lax.Precision.HIGHEST)
    rims = rims.reshape(2, row_count, 3, slab_rows, group_count, 2)
    rims = jnp.transpose(rims, (4, 0, 2, 1, 3, 5)).reshape(group_count, -1, 128)
    sent = jnp.concatenate([main, rims], axis=1)
    arrived = lax.all_to_all(sent, "mode", split_axis=0, concat_axis=0, tiled=True)
    arrived = arrived.reshape(group_count, -1)
    body = arrived[:, :main_len].reshape(MODES, halves, 2, 3, row_count, piece)
    body = jnp.transpose(body, (2, 3, 0, 1, 4, 5)).reshape(2, 3, MODES, planes, piece)
    edge = arrived[:, main_len:].reshape(MODES, halves, 2, 3, row_count * slab_rows * 2)
    edge = jnp.transpose(edge, (2, 3, 0, 1, 4)).reshape(2, 3, MODES, planes * slab_rows * 2)

    def coupled(speed, spin):
        shape = spin.shape
        mixed = [
            jnp.dot(flat_coupling, spin[c].reshape(MODES, -1), precision=lax.Precision.HIGHEST)
            .reshape((MODES, MODES) + shape[2:])
            for c in range(3)
        ]
        flux = [
            jnp.sum(speed[1][:, None] * mixed[2] - speed[2][:, None] * mixed[1], axis=0),
            jnp.sum(speed[2][:, None] * mixed[0] - speed[0][:, None] * mixed[2], axis=0),
            jnp.sum(speed[0][:, None] * mixed[1] - speed[1][:, None] * mixed[0], axis=0),
        ]
        damped = [
            jnp.dot(mixing_rows, spin[c].reshape(MODES, -1), precision=lax.Precision.HIGHEST)
            .reshape((MODES,) + shape[2:])
            for c in range(3)
        ]
        return flux, damped

    table = np.asarray(triple_table(MODES), dtype=np.float32)
    fields = pl.pallas_call(
        functools.partial(coupling_kernel, table),
        out_shape=jax.ShapeDtypeStruct((6, MODES, planes, piece), jnp.float32),
        in_specs=[pl.BlockSpec(memory_space=pltpu.SMEM), pl.BlockSpec(memory_space=pltpu.VMEM)],
        out_specs=pl.BlockSpec(memory_space=pltpu.VMEM),
        cost_estimate=pl.CostEstimate(
            flops=MODES * planes * piece * 4000,
            bytes_accessed=(6 + 6) * MODES * planes * piece * 4,
            transcendentals=0,
        ),
    )(viscosity, body)
    flux = [fields[c] for c in range(3)]
    damped = [fields[3 + c] for c in range(3)]
    flux_rim, damped_rim = coupled(edge[0], edge[1])

    count = lax.axis_size("tile")
    forward = [(i, (i + 1) % count) for i in range(count)]
    backward = [((i + 1) % count, i) for i in range(count)]
    x_needs = jnp.stack([flux[1], flux[2], damped[0], damped[1], damped[2]], axis=0)
    x_shape = x_needs[..., :chunk].shape
    low = lax.ppermute(x_needs[..., piece - chunk :].reshape(-1, 128), "tile", forward)
    high = lax.ppermute(x_needs[..., :chunk].reshape(-1, 128), "tile", backward)
    low = low.reshape(x_shape)
    high = high.reshape(x_shape)

    rims = jnp.stack(flux_rim + damped_rim, axis=0).reshape(-1, slab_rows * 2)
    lane = np.arange(piece)
    slot = (lane // chunk) * 2 + (lane % chunk == chunk - 1)
    edge_lane = (lane % chunk == 0) | (lane % chunk == chunk - 1)
    place = (np.arange(slab_rows * 2)[:, None] == slot[None, :]) & edge_lane[None, :]
    rims = jnp.dot(rims, jnp.asarray(place.astype(np.float32)), precision=lax.Precision.HIGHEST)
    rims = rims.reshape(fields.shape)
    width = piece - chunk
    halo = jnp.pad(low, ((0, 0), (0, 0), (0, 0), (0, width))) + jnp.pad(
        high, ((0, 0), (0, 0), (0, 0), (width, 0))
    )
    rate = pl.pallas_call(
        functools.partial(stencil_kernel, chunk, slab_rows),
        out_shape=jax.ShapeDtypeStruct((MODES, 3, planes, piece), jnp.float32),
        in_specs=[pl.BlockSpec(memory_space=pltpu.VMEM)] * 3,
        out_specs=pl.BlockSpec(memory_space=pltpu.VMEM),
        compiler_params=pltpu.CompilerParams(allow_input_fusion=[True, True, True]),
        cost_estimate=pl.CostEstimate(
            flops=MODES * 3 * planes * piece * 40,
            bytes_accessed=(6 + 6 + 5 + 3) * MODES * planes * piece * 4,
            transcendentals=0,
        ),
    )(fields, rims, halo)
    rate = rate.reshape(MODES, 3, halves, row_count, piece)
    rate = jnp.transpose(rate, (0, 2, 1, 3, 4)).reshape(group_count, -1, 128)
    returned = lax.all_to_all(rate, "mode", split_axis=0, concat_axis=0, tiled=True)
    returned = returned.reshape(group_count, 3, row_count, slab_rows, chunk)
    returned = jnp.transpose(returned, (2, 1, 3, 0, 4))
    return returned.reshape(row_count, 3, cell_count)


def solution(mesh):
    in_specs = (P("mode", None, "tile"), P("mode", None, "tile"), P())
    out_specs = P("mode", None, "tile")
    return jax.shard_map(shards, mesh=mesh, in_specs=in_specs, out_specs=out_specs, check_vma=False)
```

```python
import functools
import math

import jax
import jax.numpy as jnp
import numpy as np
from jax import lax
from jax.experimental import pallas as pl
from jax.experimental.pallas import tpu as pltpu
from jax.sharding import PartitionSpec as P

MODES = 8
NY = 1024


def padded(block, sides, width):
    for axis, dim in sides:
        count = lax.axis_size(axis)
        forward = [(i, i + 1) for i in range(count - 1)]
        forward.append((count - 1, 0))
        backward = [(target, source) for source, target in forward]
        low = lax.ppermute(
            lax.slice_in_dim(block, block.shape[dim] - width, None, axis=dim), axis, forward
        )
        high = lax.ppermute(lax.slice_in_dim(block, 0, width, axis=dim), axis, backward)
        block = jnp.concatenate([low, block, high], axis=dim)
    return block


def legendre_list(count, where):
    values_list = [1.0, where]
    for degree in range(1, count):
        values_list.append(
            ((2 * degree + 1) * where * values_list[degree] - degree * values_list[degree - 1])
            / (degree + 1)
        )
    return values_list


def gauss_nodes(order):
    nodes_list = []
    weights_list = []
    for number in range(order):
        guess = math.cos(math.pi * (number + 0.75) / (order + 0.5))
        for sweep in range(60):
            values_list = legendre_list(order, guess)
            slope = (
                order
                * (guess * values_list[order] - values_list[order - 1])
                / (guess * guess - 1.0)
            )
            guess = guess - values_list[order] / slope
        values_list = legendre_list(order, guess)
        slope = (
            order * (guess * values_list[order] - values_list[order - 1]) / (guess * guess - 1.0)
        )
        nodes_list.append(guess)
        weights_list.append(2.0 / ((1.0 - guess * guess) * slope * slope))
    return (nodes_list, weights_list)


def triple_table(mode_count):
    nodes_list, weights_list = gauss_nodes(2 * mode_count)
    scaled = [
        [
            math.sqrt(2.0 * degree + 1.0) * legendre_list(mode_count, node_value)[degree]
            for degree in range(mode_count)
        ]
        for node_value in nodes_list
    ]
    table = [
        [
            [
                0.5
                * sum(
                    (
                        weights_list[number]
                        * scaled[number][first]
                        * scaled[number][second]
                        * scaled[number][third]
                        for number in range(len(nodes_list))
                    )
                )
                for third in range(mode_count)
            ]
            for second in range(mode_count)
        ]
        for first in range(mode_count)
    ]
    return np.array(table)


def cross_along(left_vec, right_vec, direction):

    def component(vector, number):
        return lax.index_in_dim(vector, number, direction, keepdims=False)

    components = [
        component(left_vec, 1) * component(right_vec, 2)
        - component(left_vec, 2) * component(right_vec, 1),
        component(left_vec, 2) * component(right_vec, 0)
        - component(left_vec, 0) * component(right_vec, 2),
        component(left_vec, 0) * component(right_vec, 1)
        - component(left_vec, 1) * component(right_vec, 0),
    ]
    return jnp.stack(components, axis=direction)


def centred(source_field, direction):
    return 0.5 * (jnp.roll(source_field, -1, direction) - jnp.roll(source_field, 1, direction))


def second_diff(source_field, direction):
    return (
        jnp.roll(source_field, -1, direction)
        + jnp.roll(source_field, 1, direction)
        - 2.0 * source_field
    )


def coupling_kernel(table, visc_ref, b_ref, o_ref):
    modes = table.shape[0]
    first, second = visc_ref[0], visc_ref[1]
    mix = [
        [first * float(table[0, j, k]) + second * float(table[1, j, k]) for k in range(modes)]
        for j in range(modes)
    ]
    height = min(8, b_ref.shape[3])
    rows = b_ref.shape[3] // height
    lanes = b_ref.shape[4] // 128

    def tile(number, carry):
        zs = pl.ds(pl.multiple_of((number // lanes) * height, height), height)
        ls = pl.ds(pl.multiple_of((number % lanes) * 128, 128), 128)
        spin = [[b_ref[1, c, j, zs, ls] for c in range(3)] for j in range(modes)]
        for k in range(modes):
            total = [None, None, None]
            for i in range(modes):
                mixed = []
                for c in range(3):
                    acc = spin[0][c] * float(table[i, 0, k])
                    for j in range(1, modes):
                        acc = acc + spin[j][c] * float(table[i, j, k])
                    mixed.append(acc)
                speed = [b_ref[0, c, i, zs, ls] for c in range(3)]
                terms = [
                    speed[1] * mixed[2] - speed[2] * mixed[1],
                    speed[2] * mixed[0] - speed[0] * mixed[2],
                    speed[0] * mixed[1] - speed[1] * mixed[0],
                ]
                total = terms if i == 0 else [a + b for a, b in zip(total, terms)]
            for c in range(3):
                o_ref[c, k, zs, ls] = total[c]
                acc = spin[0][c] * mix[0][k]
                for j in range(1, modes):
                    acc = acc + spin[j][c] * mix[j][k]
                o_ref[3 + c, k, zs, ls] = acc
        return carry

    lax.fori_loop(0, rows * lanes, tile, 0)


def stencil_kernel(chunk, slab_rows, f_ref, r_ref, h_ref, o_ref):
    planes, piece = f_ref.shape[2], f_ref.shape[3]
    lane = lax.broadcasted_iota(jnp.int32, (planes, piece), 1)
    y_of = lane % chunk
    x_of = lane // chunk
    first_y = y_of == 0
    last_y = y_of == chunk - 1
    first_x = x_of == 0
    last_x = x_of == slab_rows - 1

    for k in range(f_ref.shape[1]):

        def moved(c, halo):
            f = f_ref[c, k]
            y_up = jnp.where(last_y, r_ref[c, k], pltpu.roll(f, piece - 1, 1))
            y_down = jnp.where(first_y, r_ref[c, k], pltpu.roll(f, 1, 1))
            z_up = pltpu.roll(f, planes - 1, 0)
            z_down = pltpu.roll(f, 1, 0)
            if halo is None:
                return f, y_up, y_down, z_up, z_down, None, None
            x_up = jnp.where(last_x, h_ref[halo, k], pltpu.roll(f, piece - chunk, 1))
            x_down = jnp.where(first_x, h_ref[halo, k], pltpu.roll(f, chunk, 1))
            return f, y_up, y_down, z_up, z_down, x_up, x_down

        def laplace(c):
            f, y_up, y_down, z_up, z_down, x_up, x_down = moved(3 + c, 2 + c)
            return (z_up + z_down - 2.0 * f) + (x_up + x_down - 2.0 * f) + (y_up + y_down - 2.0 * f)

        _, fx_yu, fx_yd, fx_zu, fx_zd, _, _ = moved(0, None)
        _, fy_yu, fy_yd, fy_zu, fy_zd, fy_xu, fy_xd = moved(1, 0)
        _, fz_yu, fz_yd, fz_zu, fz_zd, fz_xu, fz_xd = moved(2, 1)
        o_ref[k, 0] = 0.5 * (fz_yu - fz_yd) - 0.5 * (fy_zu - fy_zd) + laplace(0)
        o_ref[k, 1] = 0.5 * (fx_zu - fx_zd) - 0.5 * (fz_xu - fz_xd) + laplace(1)
        o_ref[k, 2] = 0.5 * (fy_xu - fy_xd) - 0.5 * (fx_yu - fx_yd) + laplace(2)


def shards(velocity, vorticity, viscosity):
    row_count = velocity.shape[0]
    cell_count = velocity.shape[2]
    slab_rows = cell_count // NY
    group_count = lax.axis_size("mode")
    chunk = NY // group_count
    piece = slab_rows * chunk
    halves = group_count // MODES
    planes = row_count * halves
    coupling = jnp.asarray(triple_table(MODES), dtype=jnp.float32)
    mixing = viscosity[0] * coupling[0] + viscosity[1] * coupling[1]
    flat_coupling = jnp.transpose(coupling, (0, 2, 1)).reshape(MODES * MODES, MODES)
    mixing_rows = jnp.transpose(mixing)

    both = jnp.stack([velocity, vorticity], axis=0).reshape(
        2, row_count, 3, slab_rows, group_count, chunk
    )
    main = jnp.transpose(both, (4, 0, 2, 1, 3, 5)).reshape(group_count, -1, 128)
    main_len = main.shape[1] * 128
    column = np.arange(NY)
    target = np.arange(group_count) * chunk
    picks = np.stack([(target - 1) % NY, (target + chunk) % NY], axis=-1).reshape(-1)
    select = jnp.asarray((column[:, None] == picks[None, :]).astype(np.float32))
    rims = jnp.dot(both.reshape(-1, NY), select, precision=lax.Precision.HIGHEST)
    rims = rims.reshape(2, row_count, 3, slab_rows, group_count, 2)
    rims = jnp.transpose(rims, (4, 0, 2, 1, 3, 5)).reshape(group_count, -1, 128)
    sent = jnp.concatenate([main, rims], axis=1)
    arrived = lax.all_to_all(sent, "mode", split_axis=0, concat_axis=0, tiled=True)
    arrived = arrived.reshape(group_count, -1)
    body = arrived[:, :main_len].reshape(MODES, halves, 2, 3, row_count, piece)
    body = jnp.transpose(body, (2, 3, 0, 1, 4, 5)).reshape(2, 3, MODES, planes, piece)
    edge = arrived[:, main_len:].reshape(MODES, halves, 2, 3, row_count * slab_rows * 2)
    edge = jnp.transpose(edge, (2, 3, 0, 1, 4)).reshape(2, 3, MODES, planes * slab_rows * 2)

    def coupled(speed, spin):
        shape = spin.shape
        mixed = [
            jnp.dot(flat_coupling, spin[c].reshape(MODES, -1), precision=lax.Precision.HIGHEST)
            .reshape((MODES, MODES) + shape[2:])
            for c in range(3)
        ]
        flux = [
            jnp.sum(speed[1][:, None] * mixed[2] - speed[2][:, None] * mixed[1], axis=0),
            jnp.sum(speed[2][:, None] * mixed[0] - speed[0][:, None] * mixed[2], axis=0),
            jnp.sum(speed[0][:, None] * mixed[1] - speed[1][:, None] * mixed[0], axis=0),
        ]
        damped = [
            jnp.dot(mixing_rows, spin[c].reshape(MODES, -1), precision=lax.Precision.HIGHEST)
            .reshape((MODES,) + shape[2:])
            for c in range(3)
        ]
        return flux, damped

    table = np.asarray(triple_table(MODES), dtype=np.float32)

    def couple(block):
        size = block.shape[3] * block.shape[4]
        return pl.pallas_call(
            functools.partial(coupling_kernel, table),
            out_shape=jax.ShapeDtypeStruct((6,) + block.shape[2:], jnp.float32),
            in_specs=[pl.BlockSpec(memory_space=pltpu.SMEM), pl.BlockSpec(memory_space=pltpu.VMEM)],
            out_specs=pl.BlockSpec(memory_space=pltpu.VMEM),
            cost_estimate=pl.CostEstimate(
                flops=MODES * size * 4000,
                bytes_accessed=(6 + 6) * MODES * size * 4,
                transcendentals=0,
            ),
        )(viscosity, block)

    fields = couple(body)
    flux = [fields[c] for c in range(3)]
    damped = [fields[3 + c] for c in range(3)]
    rim_fields = couple(edge.reshape(2, 3, MODES, 1, -1))

    count = lax.axis_size("tile")
    forward = [(i, (i + 1) % count) for i in range(count)]
    backward = [((i + 1) % count, i) for i in range(count)]
    x_needs = jnp.stack([flux[1], flux[2], damped[0], damped[1], damped[2]], axis=0)
    x_shape = x_needs[..., :chunk].shape
    low = lax.ppermute(x_needs[..., piece - chunk :].reshape(-1, 128), "tile", forward)
    high = lax.ppermute(x_needs[..., :chunk].reshape(-1, 128), "tile", backward)
    low = low.reshape(x_shape)
    high = high.reshape(x_shape)

    rims = rim_fields.reshape(-1, slab_rows * 2)
    lane = np.arange(piece)
    slot = (lane // chunk) * 2 + (lane % chunk == chunk - 1)
    edge_lane = (lane % chunk == 0) | (lane % chunk == chunk - 1)
    place = (np.arange(slab_rows * 2)[:, None] == slot[None, :]) & edge_lane[None, :]
    rims = jnp.dot(rims, jnp.asarray(place.astype(np.float32)), precision=lax.Precision.HIGHEST)
    rims = rims.reshape(fields.shape)
    width = piece - chunk
    halo = jnp.pad(low, ((0, 0), (0, 0), (0, 0), (0, width))) + jnp.pad(
        high, ((0, 0), (0, 0), (0, 0), (width, 0))
    )
    rate = pl.pallas_call(
        functools.partial(stencil_kernel, chunk, slab_rows),
        out_shape=jax.ShapeDtypeStruct((MODES, 3, planes, piece), jnp.float32),
        in_specs=[pl.BlockSpec(memory_space=pltpu.VMEM)] * 3,
        out_specs=pl.BlockSpec(memory_space=pltpu.VMEM),
        compiler_params=pltpu.CompilerParams(allow_input_fusion=[True, True, True]),
        cost_estimate=pl.CostEstimate(
            flops=MODES * 3 * planes * piece * 40,
            bytes_accessed=(6 + 6 + 5 + 3) * MODES * planes * piece * 4,
            transcendentals=0,
        ),
    )(fields, rims, halo)
    rate = rate.reshape(MODES, 3, halves, row_count, piece)
    rate = jnp.transpose(rate, (0, 2, 1, 3, 4)).reshape(group_count, -1, 128)
    returned = lax.all_to_all(rate, "mode", split_axis=0, concat_axis=0, tiled=True)
    returned = returned.reshape(group_count, 3, row_count, slab_rows, chunk)
    returned = jnp.transpose(returned, (2, 1, 3, 0, 4))
    return returned.reshape(row_count, 3, cell_count)


def solution(mesh):
    in_specs = (P("mode", None, "tile"), P("mode", None, "tile"), P())
    out_specs = P("mode", None, "tile")
    return jax.shard_map(shards, mesh=mesh, in_specs=in_specs, out_specs=out_specs, check_vma=False)
```

```python
import functools
import math

import jax
import jax.numpy as jnp
import numpy as np
from jax import lax
from jax.experimental import pallas as pl
from jax.experimental.pallas import tpu as pltpu
from jax.sharding import PartitionSpec as P

MODES = 8
NY = 1024


def padded(block, sides, width):
    for axis, dim in sides:
        count = lax.axis_size(axis)
        forward = [(i, i + 1) for i in range(count - 1)]
        forward.append((count - 1, 0))
        backward = [(target, source) for source, target in forward]
        low = lax.ppermute(
            lax.slice_in_dim(block, block.shape[dim] - width, None, axis=dim), axis, forward
        )
        high = lax.ppermute(lax.slice_in_dim(block, 0, width, axis=dim), axis, backward)
        block = jnp.concatenate([low, block, high], axis=dim)
    return block


def legendre_list(count, where):
    values_list = [1.0, where]
    for degree in range(1, count):
        values_list.append(
            ((2 * degree + 1) * where * values_list[degree] - degree * values_list[degree - 1])
            / (degree + 1)
        )
    return values_list


def gauss_nodes(order):
    nodes_list = []
    weights_list = []
    for number in range(order):
        guess = math.cos(math.pi * (number + 0.75) / (order + 0.5))
        for sweep in range(60):
            values_list = legendre_list(order, guess)
            slope = (
                order
                * (guess * values_list[order] - values_list[order - 1])
                / (guess * guess - 1.0)
            )
            guess = guess - values_list[order] / slope
        values_list = legendre_list(order, guess)
        slope = (
            order * (guess * values_list[order] - values_list[order - 1]) / (guess * guess - 1.0)
        )
        nodes_list.append(guess)
        weights_list.append(2.0 / ((1.0 - guess * guess) * slope * slope))
    return (nodes_list, weights_list)


def triple_table(mode_count):
    nodes_list, weights_list = gauss_nodes(2 * mode_count)
    scaled = [
        [
            math.sqrt(2.0 * degree + 1.0) * legendre_list(mode_count, node_value)[degree]
            for degree in range(mode_count)
        ]
        for node_value in nodes_list
    ]
    table = [
        [
            [
                0.5
                * sum(
                    (
                        weights_list[number]
                        * scaled[number][first]
                        * scaled[number][second]
                        * scaled[number][third]
                        for number in range(len(nodes_list))
                    )
                )
                for third in range(mode_count)
            ]
            for second in range(mode_count)
        ]
        for first in range(mode_count)
    ]
    return np.array(table)


def cross_along(left_vec, right_vec, direction):

    def component(vector, number):
        return lax.index_in_dim(vector, number, direction, keepdims=False)

    components = [
        component(left_vec, 1) * component(right_vec, 2)
        - component(left_vec, 2) * component(right_vec, 1),
        component(left_vec, 2) * component(right_vec, 0)
        - component(left_vec, 0) * component(right_vec, 2),
        component(left_vec, 0) * component(right_vec, 1)
        - component(left_vec, 1) * component(right_vec, 0),
    ]
    return jnp.stack(components, axis=direction)


def centred(source_field, direction):
    return 0.5 * (jnp.roll(source_field, -1, direction) - jnp.roll(source_field, 1, direction))


def second_diff(source_field, direction):
    return (
        jnp.roll(source_field, -1, direction)
        + jnp.roll(source_field, 1, direction)
        - 2.0 * source_field
    )


def coupling_kernel(table, direct, visc_ref, b_ref, o_ref):
    modes = table.shape[0]
    first, second = visc_ref[0], visc_ref[1]
    mix = [
        [first * float(table[0, j, k]) + second * float(table[1, j, k]) for k in range(modes)]
        for j in range(modes)
    ]
    if direct:
        height, rows, lanes = 8, o_ref.shape[2] // 8, o_ref.shape[3] // 128
    else:
        height = min(8, b_ref.shape[3])
        rows = b_ref.shape[3] // height
        lanes = b_ref.shape[4] // 128

    def tile(number, carry):
        zs = pl.ds(pl.multiple_of((number // lanes) * height, height), height)
        ls = pl.ds(pl.multiple_of((number % lanes) * 128, 128), 128)

        def load(kind, c, mode):
            if not direct:
                return b_ref[kind, c, mode, zs, ls]
            start = (kind * 3 + c) * height * lanes + number % lanes
            return b_ref[mode * rows + number // lanes, pl.ds(start, height, stride=lanes), :]

        spin = [[load(1, c, j) for c in range(3)] for j in range(modes)]
        for k in range(modes):
            total = [None, None, None]
            for i in range(modes):
                mixed = []
                for c in range(3):
                    acc = spin[0][c] * float(table[i, 0, k])
                    for j in range(1, modes):
                        acc = acc + spin[j][c] * float(table[i, j, k])
                    mixed.append(acc)
                speed = [load(0, c, i) for c in range(3)]
                terms = [
                    speed[1] * mixed[2] - speed[2] * mixed[1],
                    speed[2] * mixed[0] - speed[0] * mixed[2],
                    speed[0] * mixed[1] - speed[1] * mixed[0],
                ]
                total = terms if i == 0 else [a + b for a, b in zip(total, terms)]
            for c in range(3):
                o_ref[c, k, zs, ls] = total[c]
                acc = spin[0][c] * mix[0][k]
                for j in range(1, modes):
                    acc = acc + spin[j][c] * mix[j][k]
                o_ref[3 + c, k, zs, ls] = acc
        return carry

    lax.fori_loop(0, rows * lanes, tile, 0)


def stencil_kernel(chunk, slab_rows, f_ref, r_ref, h_ref, o_ref):
    planes, piece = f_ref.shape[2], f_ref.shape[3]
    lane = lax.broadcasted_iota(jnp.int32, (planes, piece), 1)
    y_of = lane % chunk
    x_of = lane // chunk
    first_y = y_of == 0
    last_y = y_of == chunk - 1
    first_x = x_of == 0
    last_x = x_of == slab_rows - 1

    for k in range(f_ref.shape[1]):

        def moved(c, halo):
            f = f_ref[c, k]
            y_up = jnp.where(last_y, r_ref[c, k], pltpu.roll(f, piece - 1, 1))
            y_down = jnp.where(first_y, r_ref[c, k], pltpu.roll(f, 1, 1))
            z_up = pltpu.roll(f, planes - 1, 0)
            z_down = pltpu.roll(f, 1, 0)
            if halo is None:
                return f, y_up, y_down, z_up, z_down, None, None
            x_up = jnp.where(last_x, h_ref[halo, k], pltpu.roll(f, piece - chunk, 1))
            x_down = jnp.where(first_x, h_ref[halo, k], pltpu.roll(f, chunk, 1))
            return f, y_up, y_down, z_up, z_down, x_up, x_down

        def laplace(c):
            f, y_up, y_down, z_up, z_down, x_up, x_down = moved(3 + c, 2 + c)
            return (z_up + z_down - 2.0 * f) + (x_up + x_down - 2.0 * f) + (y_up + y_down - 2.0 * f)

        _, fx_yu, fx_yd, fx_zu, fx_zd, _, _ = moved(0, None)
        _, fy_yu, fy_yd, fy_zu, fy_zd, fy_xu, fy_xd = moved(1, 0)
        _, fz_yu, fz_yd, fz_zu, fz_zd, fz_xu, fz_xd = moved(2, 1)
        o_ref[k, 0] = 0.5 * (fz_yu - fz_yd) - 0.5 * (fy_zu - fy_zd) + laplace(0)
        o_ref[k, 1] = 0.5 * (fx_zu - fx_zd) - 0.5 * (fz_xu - fz_xd) + laplace(1)
        o_ref[k, 2] = 0.5 * (fy_xu - fy_xd) - 0.5 * (fx_yu - fx_yd) + laplace(2)


def shards(velocity, vorticity, viscosity):
    row_count = velocity.shape[0]
    cell_count = velocity.shape[2]
    slab_rows = cell_count // NY
    group_count = lax.axis_size("mode")
    chunk = NY // group_count
    piece = slab_rows * chunk
    halves = group_count // MODES
    planes = row_count * halves
    coupling = jnp.asarray(triple_table(MODES), dtype=jnp.float32)
    mixing = viscosity[0] * coupling[0] + viscosity[1] * coupling[1]
    flat_coupling = jnp.transpose(coupling, (0, 2, 1)).reshape(MODES * MODES, MODES)
    mixing_rows = jnp.transpose(mixing)

    both = jnp.stack([velocity, vorticity], axis=0).reshape(
        2, row_count, 3, slab_rows, group_count, chunk
    )
    main = jnp.transpose(both, (4, 0, 2, 1, 3, 5)).reshape(group_count, -1, 128)
    main_len = main.shape[1] * 128
    column = np.arange(NY)
    target = np.arange(group_count) * chunk
    picks = np.stack([(target - 1) % NY, (target + chunk) % NY], axis=-1).reshape(-1)
    select = jnp.asarray((column[:, None] == picks[None, :]).astype(np.float32))
    rims = jnp.dot(both.reshape(-1, NY), select, precision=lax.Precision.HIGHEST)
    rims = rims.reshape(2, row_count, 3, slab_rows, group_count, 2)
    rims = jnp.transpose(rims, (4, 0, 2, 1, 3, 5)).reshape(group_count, -1, 128)
    sent = jnp.concatenate([main, rims], axis=1)
    arrived = lax.all_to_all(sent, "mode", split_axis=0, concat_axis=0, tiled=True)
    arrived3 = arrived
    arrived = arrived.reshape(group_count, -1)
    body = arrived[:, :main_len].reshape(MODES, halves, 2, 3, row_count, piece)
    body = jnp.transpose(body, (2, 3, 0, 1, 4, 5)).reshape(2, 3, MODES, planes, piece)
    edge = arrived[:, main_len:].reshape(MODES, halves, 2, 3, row_count * slab_rows * 2)
    edge = jnp.transpose(edge, (2, 3, 0, 1, 4)).reshape(2, 3, MODES, planes * slab_rows * 2)

    def coupled(speed, spin):
        shape = spin.shape
        mixed = [
            jnp.dot(flat_coupling, spin[c].reshape(MODES, -1), precision=lax.Precision.HIGHEST)
            .reshape((MODES, MODES) + shape[2:])
            for c in range(3)
        ]
        flux = [
            jnp.sum(speed[1][:, None] * mixed[2] - speed[2][:, None] * mixed[1], axis=0),
            jnp.sum(speed[2][:, None] * mixed[0] - speed[0][:, None] * mixed[2], axis=0),
            jnp.sum(speed[0][:, None] * mixed[1] - speed[1][:, None] * mixed[0], axis=0),
        ]
        damped = [
            jnp.dot(mixing_rows, spin[c].reshape(MODES, -1), precision=lax.Precision.HIGHEST)
            .reshape((MODES,) + shape[2:])
            for c in range(3)
        ]
        return flux, damped

    table = np.asarray(triple_table(MODES), dtype=np.float32)

    def couple(block, direct, shape):
        size = shape[1] * shape[2]
        return pl.pallas_call(
            functools.partial(coupling_kernel, table, direct),
            out_shape=jax.ShapeDtypeStruct((6,) + shape, jnp.float32),
            in_specs=[pl.BlockSpec(memory_space=pltpu.SMEM), pl.BlockSpec(memory_space=pltpu.VMEM)],
            out_specs=pl.BlockSpec(memory_space=pltpu.VMEM),
            cost_estimate=pl.CostEstimate(
                flops=MODES * size * 4000,
                bytes_accessed=(6 + 6) * MODES * size * 4,
                transcendentals=0,
            ),
        )(viscosity, block)

    fields = couple(arrived3, True, (MODES, planes, piece))
    flux = [fields[c] for c in range(3)]
    damped = [fields[3 + c] for c in range(3)]
    rim_fields = couple(edge.reshape(2, 3, MODES, 1, -1), False, (MODES, 1, edge.shape[-1]))

    count = lax.axis_size("tile")
    forward = [(i, (i + 1) % count) for i in range(count)]
    backward = [((i + 1) % count, i) for i in range(count)]
    x_needs = jnp.stack([flux[1], flux[2], damped[0], damped[1], damped[2]], axis=0)
    x_shape = x_needs[..., :chunk].shape
    low = lax.ppermute(x_needs[..., piece - chunk :].reshape(-1, 128), "tile", forward)
    high = lax.ppermute(x_needs[..., :chunk].reshape(-1, 128), "tile", backward)
    low = low.reshape(x_shape)
    high = high.reshape(x_shape)

    rims = rim_fields.reshape(-1, slab_rows * 2)
    lane = np.arange(piece)
    slot = (lane // chunk) * 2 + (lane % chunk == chunk - 1)
    edge_lane = (lane % chunk == 0) | (lane % chunk == chunk - 1)
    place = (np.arange(slab_rows * 2)[:, None] == slot[None, :]) & edge_lane[None, :]
    rims = jnp.dot(rims, jnp.asarray(place.astype(np.float32)), precision=lax.Precision.HIGHEST)
    rims = rims.reshape(fields.shape)
    width = piece - chunk
    halo = jnp.pad(low, ((0, 0), (0, 0), (0, 0), (0, width))) + jnp.pad(
        high, ((0, 0), (0, 0), (0, 0), (width, 0))
    )
    rate = pl.pallas_call(
        functools.partial(stencil_kernel, chunk, slab_rows),
        out_shape=jax.ShapeDtypeStruct((MODES, 3, planes, piece), jnp.float32),
        in_specs=[pl.BlockSpec(memory_space=pltpu.VMEM)] * 3,
        out_specs=pl.BlockSpec(memory_space=pltpu.VMEM),
        compiler_params=pltpu.CompilerParams(allow_input_fusion=[True, True, True]),
        cost_estimate=pl.CostEstimate(
            flops=MODES * 3 * planes * piece * 40,
            bytes_accessed=(6 + 6 + 5 + 3) * MODES * planes * piece * 4,
            transcendentals=0,
        ),
    )(fields, rims, halo)
    rate = rate.reshape(MODES, 3, halves, row_count, piece)
    rate = jnp.transpose(rate, (0, 2, 1, 3, 4)).reshape(group_count, -1, 128)
    returned = lax.all_to_all(rate, "mode", split_axis=0, concat_axis=0, tiled=True)
    returned = returned.reshape(group_count, 3, row_count, slab_rows, chunk)
    returned = jnp.transpose(returned, (2, 1, 3, 0, 4))
    return returned.reshape(row_count, 3, cell_count)


def solution(mesh):
    in_specs = (P("mode", None, "tile"), P("mode", None, "tile"), P())
    out_specs = P("mode", None, "tile")
    return jax.shard_map(shards, mesh=mesh, in_specs=in_specs, out_specs=out_specs, check_vma=False)
```
